32 devices in a mesh: groups: 2 (over x), section: 16 (over z, y, core).
Axes of the slice: x: 2, y: 2, z: 4, core: 2. Of those that a mesh axis runs over, the one named last changes fastest.
Arguments:
- hidden_in: bfloat16 [512, 3072], P(('groups', 'section')), parts along dimension 0, may hold values from -0.59765625 to 0.59765625
- latent_in: bfloat16 [512, 64], P(('groups', 'section')), parts along dimension 0, may hold values from -6 to 6
- w_qkv: bfloat16 [3, 3072, 6144], P(None, None, 'section'), may hold values from -0.109375 to 0.109375
- w_out: bfloat16 [6144, 3072], P('section'), may hold values from -0.109375 to 0.109375
- stale_kv: bfloat16 [4, 256, 6144], P('groups', None, 'section'), parts along dimension 0, may hold values from -3 to 3
- qk_gain: float32 [2, 2, 128], replicated, may hold values from 0.6 to 2.4
- block_mod: float32 [4, 3, 3072], P('groups'), parts along dimension 0, may hold values from -4 to 4
- final_mod: float32 [4, 3072], P('groups'), parts along dimension 0, may hold values from -3 to 3
- w_final: bfloat16 [3072, 64], replicated, may hold values from -0.109375 to 0.109375
- w_embed: bfloat16 [64, 3072], replicated, may hold values from -0.75 to 0.75
- patch_flow: int32 [6, 2], replicated, may hold values from 0 to 1, as said below
Outputs:
- hidden_out: bfloat16 [512, 3072], P(('groups', 'section')), parts along dimension 0
- latent_out: bfloat16 [512, 64], P(('groups', 'section')), parts along dimension 0
The draws below stay inside these ranges and needn't reach their ends.
There are 2 independent parts, one for each index of `groups`. The reference program is written for one: setup_inputs(seed, part) draws one part's arguments, and reference() takes and returns one part's arrays. A program takes and returns all parts, laid end to end along the dimension named above; an argument that names none is the same for every part. Nothing has to cross between parts.
Inputs may be any that keep to these rules, and one draw needn't show every extreme that they name: `patch_flow`: each row holds each of 0 to 1 once.
All inputs are finite; a program needn't handle non-finite values.
Results may differ from the reference program's by a relative error of at most 0.03.
Values may be sent and summed in bfloat16 or wider, within the bound.
No kernel may reach another device: no remote copies, remote signals or barrier semaphores. Data moves between devices by JAX's collectives and lax.ppermute only.
A program may use at most 128 MiB of HBM per device.

```python
import math
import jax
import jax.numpy as jnp
from jax import lax

D = 3072
HS = 128
C = 64
HEADS = 24
TICKS = 6
PT = 128
SECTIONS = 2
TOTAL = 256


def draw_patch_flow(key, part):

    def one_row(row_index):
        return jax.random.permutation(jax.random.fold_in(key, 7001 + row_index), SECTIONS).astype(jnp.int32)
    return jax.vmap(one_row)(jnp.arange(TICKS, dtype=jnp.int32))


def draw_block_mod(key, part):
    shift_scale = jnp.clip(0.8 * jax.random.normal(jax.random.fold_in(key, 11), (SECTIONS, 2, D), jnp.float32), -3.2, 3.2)
    large_gate = jax.random.uniform(jax.random.fold_in(key, 13), (SECTIONS, D), jnp.float32, 2.5, 4.0)
    small_gate = jax.random.uniform(jax.random.fold_in(key, 17), (SECTIONS, D), jnp.float32, 0.1, 0.13)
    sign_bits = jax.random.randint(jax.random.fold_in(key, 19), (SECTIONS, D), 0, 2)
    signs = (2 * sign_bits - 1).astype(jnp.float32)
    large_count = max(D // 10, 1)

    def ranks(section_index):
        return jax.random.permutation(jax.random.fold_in(key, 5003 + section_index), D).astype(jnp.int32)
    order = jax.vmap(ranks)(jnp.arange(SECTIONS, dtype=jnp.int32))
    is_large = order < large_count
    gate = signs * jnp.where(is_large, large_gate, small_gate)
    return jnp.concatenate([shift_scale, gate[:, None, :]], axis=1).astype(jnp.float32)


def steps_of(rng, dims, cuts, low, top_value):
    loudness = 1.0
    for dim, parts in cuts:
        draws = jax.random.uniform(jax.random.fold_in(jax.random.fold_in(rng, 6), dim), (parts,), jnp.float32, low / len(cuts), top_value / len(cuts))
        loudness = loudness * jnp.repeat(jnp.exp(draws), dims[dim] // parts).reshape((-1,) + (1,) * (len(dims) - 1 - dim))
    return loudness


def scatter_about(key, extent, scale, most, shards=(), held_as=jnp.bfloat16):
    values = jax.random.normal(key, extent, jnp.float32) * scale
    if len(shards) > 0:
        values = steps_of(key, extent, shards, -0.22, 0.18) * values
    return jnp.clip(values, min=-most, max=most).astype(held_as)


def setup_inputs(seed: int = 0, part: int = 0) -> dict:
    key_of = jax.random.split(jax.random.key(seed), 12)
    part_splits = jax.random.split(jax.random.fold_in(key_of[11], part), 12)
    return {
        "hidden_in": scatter_about(part_splits[0], (TOTAL, D), 0.1, 0.59765625, ((0, 16),)),
        "latent_in": scatter_about(part_splits[1], (TOTAL, C), 1.0, 6.0, ((0, 16),)),
        "w_qkv": scatter_about(key_of[2], (3, D, SECTIONS * HEADS * HS), D ** -0.5, 0.109375, ((2, 16),)),
        "w_out": scatter_about(key_of[3], (SECTIONS * HEADS * HS, D), (HEADS * HS) ** -0.5, 0.109375, ((0, 16),)),
        "stale_kv": jnp.clip(jax.random.uniform(part_splits[4], (2, TOTAL, SECTIONS * HEADS * HS), jnp.float32, -3.0, 3.0) * steps_of(part_splits[4], (2, TOTAL, SECTIONS * HEADS * HS), ((2, 16),), -0.4, 0.0), -3.0, 3.0).astype(jnp.bfloat16),
        "qk_gain": jnp.clip(jnp.exp(jax.random.uniform(key_of[5], (SECTIONS, 2, HS), jnp.float32, math.log(0.6), math.log(2.4))), 0.6, 2.4),
        "block_mod": draw_block_mod(jax.random.fold_in(jax.random.fold_in(key_of[11], part), 71), part),
        "final_mod": scatter_about(part_splits[7], (2, D), 0.5, 3.0, (), jnp.float32),
        "w_final": scatter_about(key_of[8], (D, C), D ** -0.5, 0.109375),
        "w_embed": scatter_about(key_of[9], (C, D), C ** -0.5, 0.75),
        "patch_flow": draw_patch_flow(jax.random.fold_in(key_of[11], 71), part),
    }


def as_float(array):
    return lax.optimization_barrier(array).astype(jnp.float32)

def layer_norm(tokens, offset_row, scale_row):
    average = lax.optimization_barrier(jnp.mean(tokens, axis=-1, keepdims=True))
    centred = tokens - average
    variance = lax.optimization_barrier(jnp.mean(centred * centred, axis=-1, keepdims=True))
    return (centred * lax.rsqrt(variance + 1e-06) * (1.0 + scale_row) + offset_row).astype(jnp.bfloat16)

def head_norm(values, gain_row):
    return (values * lax.rsqrt(lax.optimization_barrier(jnp.mean(values * values, axis=-1, keepdims=True)) + 1e-06) * gain_row).astype(jnp.bfloat16)

def section_block(hidden, weights_qkv, weights_out, key_cache, value_cache, modulation, norm_gains, patch_index):
    token_count = hidden.shape[0]
    total_rows = key_cache.shape[0]
    normed = layer_norm(hidden.astype(jnp.float32), modulation[0], modulation[1])
    queries = jnp.dot(normed, weights_qkv[0], preferred_element_type=jnp.float32).reshape(token_count, HEADS, HS)
    fresh_keys = jnp.dot(normed, weights_qkv[1], preferred_element_type=jnp.float32).reshape(token_count, HEADS, HS)
    fresh_values = jnp.dot(normed, weights_qkv[2], preferred_element_type=jnp.float32)
    query_norm = head_norm(queries, norm_gains[0])
    key_norm = head_norm(fresh_keys, norm_gains[1]).reshape(token_count, HEADS * HS)
    offset = (patch_index * token_count).astype(jnp.int32)
    key_cache = lax.dynamic_update_slice(key_cache, key_norm, (offset, jnp.int32(0)))
    value_cache = lax.dynamic_update_slice(value_cache, fresh_values.astype(jnp.bfloat16), (offset, jnp.int32(0)))
    scores = jnp.einsum('qhd,khd->hqk', as_float(query_norm), as_float(key_cache).reshape(total_rows, HEADS, HS)) / math.sqrt(HS)
    exp_scores = jnp.exp(scores)
    totals = lax.optimization_barrier(jnp.sum(exp_scores, axis=-1))
    attended = jnp.einsum('hqk,khd->qhd', as_float(exp_scores.astype(jnp.bfloat16)), as_float(value_cache).reshape(total_rows, HEADS, HS))
    attended = (attended / jnp.transpose(totals)[:, :, None]).astype(jnp.bfloat16).reshape(token_count, HEADS * HS)
    projected = jnp.dot(attended, weights_out, preferred_element_type=jnp.float32)
    result = (hidden.astype(jnp.float32) + modulation[2] * projected).astype(jnp.bfloat16)
    return (result, key_cache, value_cache)

def restart(hidden, latent, final_mod, w_final, w_embed):
    normed = layer_norm(hidden.astype(jnp.float32), final_mod[0], final_mod[1])
    velocity = jnp.dot(normed, w_final, preferred_element_type=jnp.float32)
    renewed = (latent.astype(jnp.float32) + velocity).astype(jnp.bfloat16)
    embedded = jnp.dot(renewed, w_embed, preferred_element_type=jnp.float32).astype(jnp.bfloat16)
    return (embedded, renewed)

def reference(hidden_in, latent_in, w_qkv, w_out, stale_kv, qk_gain, block_mod, final_mod, w_final, w_embed, patch_flow):
    width = HEADS * HS
    hidden = hidden_in.reshape(SECTIONS, PT, D)
    latent = latent_in.reshape(SECTIONS, PT, C)
    section_qkv = jnp.transpose(w_qkv.reshape(3, D, SECTIONS, width), (2, 0, 1, 3))
    section_out = w_out.reshape(SECTIONS, width, D)
    caches = jnp.transpose(stale_kv.reshape(2, TOTAL, SECTIONS, width), (2, 0, 1, 3))
    key_cache = caches[:, 0]
    value_cache = caches[:, 1]
    block = jax.vmap(section_block)
    for tick_index in range(TICKS):
        patches = patch_flow[tick_index]
        hidden, key_cache, value_cache = block(hidden, section_qkv, section_out, key_cache, value_cache, block_mod, qk_gain, patches)
        hidden = jnp.roll(hidden, 1, axis=0)
        latent = jnp.roll(latent, 1, axis=0)
        start_hidden, start_latent = restart(hidden[0], latent[0], final_mod, w_final, w_embed)
        hidden = hidden.at[0].set(start_hidden)
        latent = latent.at[0].set(start_latent)
    return (hidden.reshape(TOTAL, D), latent.reshape(TOTAL, C))
```

```python
import functools
import math

import jax
import jax.numpy as jnp
from jax import lax
from jax.experimental import pallas as pl
from jax.experimental.pallas import tpu as pltpu
from jax.sharding import PartitionSpec as P

HS = 128
GROUP = 8
VMEM = pltpu.VMEM
SMEM = pltpu.SMEM
EPS = 1e-6


def f32(value):
    return value.astype(jnp.float32)


def layer_norm(tokens, offset_row, scale_row):
    average = jnp.mean(tokens, axis=-1, keepdims=True)
    centred = tokens - average
    variance = jnp.mean(centred * centred, axis=-1, keepdims=True)
    return (centred * lax.rsqrt(variance + EPS) * (1.0 + scale_row) + offset_row).astype(
        jnp.bfloat16
    )


def dot(left, right):
    return jnp.dot(left, right, preferred_element_type=jnp.float32)


def block_kernel(with_latent, refs):
    if with_latent:
        (flags, own, other, latent, w_embed, mod, gains, w_qkv, w_out, k_in, v_in) = refs[:11]
        (kept, sent, k_cache, v_cache, normed, attended) = refs[11:]
    else:
        (flags, own, other, gains, w_qkv, w_out, k_in, v_in) = refs[:8]
        (kept, sent, k_cache, v_cache, normed, attended) = refs[8:]
    half = own.shape[0]
    rows = 2 * half
    heads = w_out.shape[0] // HS

    def take_rows():
        normed[:half, :] = own[...]
        normed[half:, :] = other[...]

    if with_latent:
        first = flags[0] == 0

        @pl.when(first)
        def _():
            hidden = f32(dot(latent[...], w_embed[...]).astype(jnp.bfloat16))
            normed[...] = layer_norm(hidden, mod[0:1, :], mod[1:2, :])

        pl.when(jnp.logical_not(first))(take_rows)
    else:
        take_rows()

    start = pl.multiple_of(flags[1] * rows, rows)
    k_cache[...] = k_in[...]
    v_cache[...] = v_in[...]

    def head_norm(values, gain_row):
        power = jnp.mean(values * values, axis=-1, keepdims=True)
        return (values * lax.rsqrt(power + EPS) * gain_row).astype(jnp.bfloat16)

    tokens = normed[...]
    keys = dot(tokens, w_qkv[1])
    for head in range(heads):
        part = slice(head * HS, (head + 1) * HS)
        k_cache[pl.ds(start, rows), part] = head_norm(keys[:, part], gains[1:2, :])
    v_cache[pl.ds(start, rows), :] = dot(tokens, w_qkv[2]).astype(jnp.bfloat16)
    queries = dot(tokens, w_qkv[0])
    for head in range(heads):
        part = slice(head * HS, (head + 1) * HS)
        query = head_norm(queries[:, part], gains[0:1, :])
        scores = lax.dot_general(
            query, k_cache[:, part], (((1,), (1,)), ((), ())), preferred_element_type=jnp.float32
        ) / math.sqrt(HS)
        weights = jnp.exp(scores)
        totals = jnp.sum(weights, axis=-1, keepdims=True)
        mixed = dot(weights.astype(jnp.bfloat16), v_cache[:, part])
        attended[:, part] = (mixed / totals).astype(jnp.bfloat16)
    width = w_out.shape[1]
    tile = width // 4
    heads_out = attended[...]
    for low in range(0, width, tile):
        projected = dot(heads_out, w_out[:, low : low + tile])
        kept[:, low : low + tile] = projected[:half, :]
        sent[:, low : low + tile] = projected[half:, :].astype(jnp.bfloat16)


def block(flags, own, other, latent, w_embed, mod, gains, w_qkv, w_out, k_cache, v_cache):
    half, width = own.shape
    columns = w_out.shape[0]
    with_latent = latent is not None
    args = [flags, own, other]
    if with_latent:
        args += [latent, w_embed, mod]
    args += [gains, w_qkv, w_out, k_cache, v_cache]
    count = len(args)
    flops = 2 * 2 * half * columns * width * 4
    whole = pl.BlockSpec(memory_space=VMEM)
    return pl.pallas_call(
        lambda *refs: block_kernel(with_latent, refs),
        out_shape=(
            jax.ShapeDtypeStruct((half, width), jnp.float32),
            jax.ShapeDtypeStruct((half, width), jnp.bfloat16),
            jax.ShapeDtypeStruct(k_cache.shape, jnp.bfloat16),
            jax.ShapeDtypeStruct(v_cache.shape, jnp.bfloat16),
        ),
        in_specs=[pl.BlockSpec(memory_space=SMEM)] + [whole] * (count - 1),
        out_specs=(whole,) * 4,
        scratch_shapes=[
            VMEM((2 * half, width), jnp.bfloat16),
            VMEM((2 * half, columns), jnp.bfloat16),
        ],
        input_output_aliases={count - 2: 2, count - 1: 3},
        compiler_params=pltpu.CompilerParams(vmem_limit_bytes=32 * 1024 * 1024),
        cost_estimate=pl.CostEstimate(
            flops=flops, bytes_accessed=4 * columns * width * 2, transcendentals=0
        ),
        name="block",
    )(*args)


def result_kernel(with_latent, refs):
    flags, kept, came, hidden, latent, gate, w_embed, out = refs

    def finish(base):
        out[...] = (base + gate[2:3, :] * (kept[...] + f32(came[...]))).astype(jnp.bfloat16)

    if with_latent:
        first = flags[0] == 0

        @pl.when(first)
        def _():
            finish(f32(dot(latent[...], w_embed[...]).astype(jnp.bfloat16)))

        @pl.when(jnp.logical_not(first))
        def _():
            finish(f32(hidden[...]))
    else:
        finish(f32(hidden[...]))


def result_rows(with_latent, flags, kept, came, hidden, latent, mod, w_embed):
    whole = pl.BlockSpec(memory_space=VMEM)
    return pl.pallas_call(
        lambda *refs: result_kernel(with_latent, refs),
        out_shape=jax.ShapeDtypeStruct(hidden.shape, jnp.bfloat16),
        in_specs=[pl.BlockSpec(memory_space=SMEM)] + [whole] * 6,
        out_specs=whole,
        compiler_params=pltpu.CompilerParams(vmem_limit_bytes=8 * 1024 * 1024),
        name="result",
    )(flags, kept, came, hidden, latent, mod, w_embed)


def renew_kernel(flags, kept, came, hidden, latent, mod, final_mod, w_final, out):
    last = flags[2] == 1

    @pl.when(last)
    def _():
        total = f32(hidden[...]) + mod[2:3, :] * (kept[...] + f32(came[...]))
        total = f32(total.astype(jnp.bfloat16))
        normed = layer_norm(total, final_mod[0:1, :], final_mod[1:2, :])
        velocity = dot(normed, w_final[...])
        out[...] = (f32(latent[...]) + velocity).astype(jnp.bfloat16)

    @pl.when(jnp.logical_not(last))
    def _():
        out[...] = latent[...]


def renew(flags, kept, came, hidden, latent, mod, final_mod, w_final):
    whole = pl.BlockSpec(memory_space=VMEM)
    return pl.pallas_call(
        renew_kernel,
        out_shape=jax.ShapeDtypeStruct(latent.shape, jnp.bfloat16),
        in_specs=[pl.BlockSpec(memory_space=SMEM)] + [whole] * 7,
        out_specs=whole,
        compiler_params=pltpu.CompilerParams(vmem_limit_bytes=8 * 1024 * 1024),
        name="renew",
    )(flags, kept, came, hidden, latent, mod, final_mod, w_final)


def norm_kernel(hidden, mod, out):
    out[...] = layer_norm(f32(hidden[...]), mod[0:1, :], mod[1:2, :])


def norm_rows(hidden, mod):
    whole = pl.BlockSpec(memory_space=VMEM)
    return pl.pallas_call(
        norm_kernel,
        out_shape=jax.ShapeDtypeStruct(hidden.shape, jnp.bfloat16),
        in_specs=[whole] * 2,
        out_specs=whole,
        compiler_params=pltpu.CompilerParams(vmem_limit_bytes=8 * 1024 * 1024),
        name="norm",
    )(hidden, mod)


def chip_partner(device, stage):
    return device ^ (4 if (device & 1) == stage else 2)


def routes(devices, partner_of):
    return [(device, partner_of(device)) for device in devices]


def send(value, route):
    return lax.ppermute(value, "section", route)


def stack(upper, lower):
    return jnp.concatenate([upper, lower], 0)


def gather_chips(rows, devices):
    rows = stack(rows, send(rows, routes(devices, lambda d: chip_partner(d, 1))))
    return stack(rows, send(rows, routes(devices, lambda d: chip_partner(d, 0))))


def reduce_rows(kept, sent, devices):
    kept = kept + f32(send(sent, routes(devices, lambda d: d ^ 1)))
    for stage in range(2):
        half = kept.shape[0] // 2
        came = send(
            kept[half:].astype(jnp.bfloat16), routes(devices, lambda d: chip_partner(d, stage))
        )
        if stage == 1:
            return (kept[:half], came)
        kept = kept[:half] + f32(came)


def body(
    hidden_in,
    latent_in,
    w_qkv,
    w_out,
    stale_kv,
    qk_gain,
    block_mod,
    final_mod,
    w_final,
    w_embed,
    patch_flow,
):
    size = lax.axis_size("section")
    ticks = patch_flow.shape[0]
    everyone = range(size)
    head, tail = range(GROUP), range(size - GROUP, size)
    front, rest = range(size - GROUP), range(GROUP, size)
    section = lax.axis_index("section") // GROUP
    is_last = (section == size // GROUP - 1).astype(jnp.int32)
    mod = lax.dynamic_index_in_dim(block_mod, section, 0, keepdims=False)
    gains = lax.dynamic_index_in_dim(qk_gain, section, 0, keepdims=False)
    patches = lax.dynamic_index_in_dim(patch_flow, section, 1, keepdims=False)
    k_cache, v_cache = stale_kv[0], stale_kv[1]

    hidden, latent = hidden_in, latent_in
    for tick in range(ticks):
        flags = jnp.stack([section.astype(jnp.int32), patches[tick], is_last])
        later = tick > 0
        own = gather_chips(norm_rows(hidden, mod), rest if later else everyone)
        other = send(own, routes(rest if later else everyone, lambda d: d ^ 1))
        latents = None
        if later:
            latents = gather_chips(latent, head)
            latents = stack(latents, send(latents, routes(head, lambda d: d ^ 1)))
        kept, sent, k_cache, v_cache = block(
            flags, own, other, latents, w_embed, mod, gains, w_qkv, w_out, k_cache, v_cache
        )
        total, came = reduce_rows(kept, sent, front)
        result = result_rows(later, flags, total, came, hidden, latent, mod, w_embed)
        moved = send(result, routes(front, lambda d: d + GROUP))
        kept, sent, result = lax.optimization_barrier((kept, sent, result))
        total, came = reduce_rows(kept, sent, tail)
        latent = renew(flags, total, came, hidden, latent, mod, final_mod, w_final)
        latent = send(latent, routes(everyone, lambda d: (d + GROUP) % size))
        hidden = moved
    embedded = dot(latent, w_embed).astype(jnp.bfloat16)
    return (jnp.where(section == 0, embedded, hidden), latent)


def solution(mesh):
    in_specs = (
        P(("groups", "section"), None),
        P(("groups", "section"), None),
        P(None, None, "section"),
        P("section", None),
        P("groups", None, "section"),
        P(),
        P("groups", None, None),
        P("groups", None),
        P(),
        P(),
        P(),
    )
    out_specs = (P(("groups", "section"), None), P(("groups", "section"), None))
    return jax.shard_map(body, mesh=mesh, in_specs=in_specs, out_specs=out_specs, check_vma=False)
```

```python
import functools
import math

import jax
import jax.numpy as jnp
from jax import lax
from jax.experimental import pallas as pl
from jax.experimental.pallas import tpu as pltpu
from jax.sharding import PartitionSpec as P

HS = 128
GROUP = 8
VMEM = pltpu.VMEM
SMEM = pltpu.SMEM
EPS = 1e-6
CHIPS = 4
CHIP_STEPS = (6, 4, 2)
BLOCK_MIB = 8


def f32(value):
    return value.astype(jnp.float32)


def layer_norm(tokens, offset_row, scale_row):
    average = jnp.mean(tokens, axis=-1, keepdims=True)
    centred = tokens - average
    variance = jnp.mean(centred * centred, axis=-1, keepdims=True)
    return (centred * lax.rsqrt(variance + EPS) * (1.0 + scale_row) + offset_row).astype(
        jnp.bfloat16
    )


def dot(left, right):
    return jnp.dot(left, right, preferred_element_type=jnp.float32)


WHOLE = pl.BlockSpec(memory_space=VMEM)
SCALARS = pl.BlockSpec(memory_space=SMEM)
LANES = 128


def params(mebibytes):
    return pltpu.CompilerParams(vmem_limit_bytes=mebibytes * 1024 * 1024)


def block_kernel(
    flags, own, other, gains, w_qkv, w_out, k_in, v_in, kept, sent, k_cache, v_cache, normed, attended
):
    half = own.shape[0]
    rows = 2 * half
    heads = w_out.shape[0] // HS
    normed[:half, :] = own[...]
    normed[half:, :] = other[...]
    start = pl.multiple_of(flags[1] * rows, rows)
    k_cache[...] = k_in[...]
    v_cache[...] = v_in[...]

    def head_norm(values, gain_row):
        power = jnp.mean(values * values, axis=-1, keepdims=True)
        return (values * lax.rsqrt(power + EPS) * gain_row).astype(jnp.bfloat16)

    tokens = normed[...]
    keys = dot(tokens, w_qkv[1])
    for head in range(heads):
        part = slice(head * HS, (head + 1) * HS)
        k_cache[pl.ds(start, rows), part] = head_norm(keys[:, part], gains[1:2, :])
    v_cache[pl.ds(start, rows), :] = dot(tokens, w_qkv[2]).astype(jnp.bfloat16)
    queries = dot(tokens, w_qkv[0])
    for head in range(heads):
        part = slice(head * HS, (head + 1) * HS)
        query = head_norm(queries[:, part], gains[0:1, :])
        scores = lax.dot_general(
            query, k_cache[:, part], (((1,), (1,)), ((), ())), preferred_element_type=jnp.float32
        ) / math.sqrt(HS)
        weights = jnp.exp(scores)
        totals = jnp.sum(weights, axis=-1, keepdims=True)
        mixed = dot(weights.astype(jnp.bfloat16), v_cache[:, part])
        attended[:, part] = (mixed / totals).astype(jnp.bfloat16)
    width = w_out.shape[1]
    tile = width // 4
    heads_out = attended[...]
    for low in range(0, width, tile):
        projected = dot(heads_out, w_out[:, low : low + tile])
        kept[:, low : low + tile] = projected[:half, :]
        sent[:, low : low + tile] = projected[half:, :].astype(jnp.bfloat16)


def block(flags, own, other, gains, w_qkv, w_out, k_cache, v_cache):
    half, width = own.shape
    columns = w_out.shape[0]
    return pl.pallas_call(
        block_kernel,
        out_shape=(
            jax.ShapeDtypeStruct((half, width), jnp.float32),
            jax.ShapeDtypeStruct((half, width), jnp.bfloat16),
            jax.ShapeDtypeStruct(k_cache.shape, jnp.bfloat16),
            jax.ShapeDtypeStruct(v_cache.shape, jnp.bfloat16),
        ),
        in_specs=[SCALARS] + [WHOLE] * 7,
        out_specs=(WHOLE,) * 4,
        scratch_shapes=[
            VMEM((2 * half, width), jnp.bfloat16),
            VMEM((2 * half, columns), jnp.bfloat16),
        ],
        input_output_aliases={6: 2, 7: 3},
        compiler_params=params(BLOCK_MIB),
        cost_estimate=pl.CostEstimate(
            flops=16 * half * columns * width,
            bytes_accessed=8 * columns * width,
            transcendentals=0,
        ),
        name="block",
    )(flags, own, other, gains, w_qkv, w_out, k_cache, v_cache)


def split_kernel(kept, came, mine, *others):
    rows = mine.shape[0]
    mine[...] = kept[:rows, :] + f32(came[:rows, :])
    for place, out in enumerate(others):
        part = slice((place + 1) * rows, (place + 2) * rows)
        out[...] = (kept[part, :] + f32(came[part, :])).astype(jnp.bfloat16)


def split(kept, came):
    rows, width = kept.shape[0] // CHIPS, kept.shape[1]
    return pl.pallas_call(
        split_kernel,
        out_shape=(jax.ShapeDtypeStruct((rows, width), jnp.float32),)
        + (jax.ShapeDtypeStruct((rows, width), jnp.bfloat16),) * (CHIPS - 1),
        in_specs=[WHOLE] * 2,
        out_specs=(WHOLE,) * CHIPS,
        compiler_params=params(4),
        name="split",
    )(kept, came)


def finish_kernel(
    flags, mine, one, two, three, hidden, latent, mod, final_mod, w_final, w_embed, packet
):
    rows, width = mine.shape
    channels = latent.shape[1]
    total = mine[...] + f32(one[...]) + f32(two[...]) + f32(three[...])
    result = (f32(hidden[...]) + mod[2:3, :] * total).astype(jnp.bfloat16)
    last = flags[2] == 1

    @pl.when(last)
    def _():
        normed = layer_norm(f32(result), final_mod[0:1, :], final_mod[1:2, :])
        velocity = dot(normed, w_final[...])
        renewed = (f32(latent[...]) + velocity).astype(jnp.bfloat16)
        packet[:, :width] = dot(renewed, w_embed[...]).astype(jnp.bfloat16)
        packet[:, width : width + channels] = renewed

    @pl.when(jnp.logical_not(last))
    def _():
        packet[:, :width] = result
        packet[:, width : width + channels] = latent[...]


def finish(flags, parts, hidden, latent, mod, final_mod, w_final, w_embed):
    rows, width = hidden.shape
    return pl.pallas_call(
        finish_kernel,
        out_shape=jax.ShapeDtypeStruct((rows, width + LANES), jnp.bfloat16),
        in_specs=[SCALARS] + [WHOLE] * 10,
        out_specs=WHOLE,
        compiler_params=params(4),
        name="finish",
    )(flags, *parts, hidden, latent, mod, final_mod, w_final, w_embed)


def norm_kernel(packet, mod, hidden, latent, normed):
    width = hidden.shape[1]
    values = packet[:, :width]
    hidden[...] = values
    latent[...] = packet[:, width : width + latent.shape[1]]
    normed[...] = layer_norm(f32(values), mod[0:1, :], mod[1:2, :])


def open_packet(packet, mod, channels):
    rows, width = packet.shape[0], packet.shape[1] - LANES
    return pl.pallas_call(
        norm_kernel,
        out_shape=(
            jax.ShapeDtypeStruct((rows, width), jnp.bfloat16),
            jax.ShapeDtypeStruct((rows, channels), jnp.bfloat16),
            jax.ShapeDtypeStruct((rows, width), jnp.bfloat16),
        ),
        in_specs=[WHOLE] * 2,
        out_specs=(WHOLE,) * 3,
        compiler_params=params(4),
        name="norm",
    )(packet, mod)


def exchange(value, apart):
    route = [(device, device ^ apart) for device in range(lax.axis_size("section"))]
    return lax.ppermute(value, "section", route)


def gather_chips(rows):
    return jnp.concatenate([rows] + [exchange(rows, apart) for apart in CHIP_STEPS], 0)


def body(
    hidden_in,
    latent_in,
    w_qkv,
    w_out,
    stale_kv,
    qk_gain,
    block_mod,
    final_mod,
    w_final,
    w_embed,
    patch_flow,
):
    size = lax.axis_size("section")
    ticks = patch_flow.shape[0]
    channels = latent_in.shape[1]
    section = lax.axis_index("section") // GROUP
    is_last = (section == size // GROUP - 1).astype(jnp.int32)
    mod = lax.dynamic_index_in_dim(block_mod, section, 0, keepdims=False)
    gains = lax.dynamic_index_in_dim(qk_gain, section, 0, keepdims=False)
    patches = lax.dynamic_index_in_dim(patch_flow, section, 1, keepdims=False)
    k_cache, v_cache = stale_kv[0], stale_kv[1]
    onward = [(device, (device + GROUP) % size) for device in range(size)]

    packet = jnp.pad(
        jnp.concatenate([hidden_in, latent_in], 1), ((0, 0), (0, LANES - channels))
    )
    for tick in range(ticks):
        flags = jnp.stack([section.astype(jnp.int32), patches[tick], is_last])
        hidden, latent, normed = open_packet(packet, mod, channels)
        own = gather_chips(normed)
        other = exchange(own, 1)
        kept, sent, k_cache, v_cache = block(
            flags, own, other, gains, w_qkv, w_out, k_cache, v_cache
        )
        mine, *blocks = split(kept, exchange(sent, 1))
        parts = [mine] + [exchange(rows, apart) for rows, apart in zip(blocks, CHIP_STEPS)]
        packet = finish(flags, parts, hidden, latent, mod, final_mod, w_final, w_embed)
        packet = lax.ppermute(packet, "section", onward)
    width = hidden_in.shape[1]
    return (packet[:, :width], packet[:, width : width + channels])


def solution(mesh):
    in_specs = (
        P(("groups", "section"), None),
        P(("groups", "section"), None),
        P(None, None, "section"),
        P("section", None),
        P("groups", None, "section"),
        P(),
        P("groups", None, None),
        P("groups", None),
        P(),
        P(),
        P(),
    )
    out_specs = (P(("groups", "section"), None), P(("groups", "section"), None))
    return jax.shard_map(body, mesh=mesh, in_specs=in_specs, out_specs=out_specs, check_vma=False)
```

```python
import functools
import math

import jax
import jax.numpy as jnp
from jax import lax
from jax.experimental import pallas as pl
from jax.experimental.pallas import tpu as pltpu
from jax.sharding import PartitionSpec as P

HS = 128
GROUP = 8
CHIPS = 4
CHIP_STEPS = (6, 4, 2)
LANES = 128
EPS = 1e-6
VMEM = pltpu.VMEM
WHOLE = pl.BlockSpec(memory_space=pltpu.VMEM)
SCALARS = pl.BlockSpec(memory_space=pltpu.SMEM)


def f32(value):
    return value.astype(jnp.float32)


def dot(left, right):
    return jnp.dot(left, right, preferred_element_type=jnp.float32)


def dot_rows(left, right):
    return lax.dot_general(
        left, right, (((1,), (1,)), ((), ())), preferred_element_type=jnp.float32
    )


def params(mebibytes):
    return pltpu.CompilerParams(vmem_limit_bytes=mebibytes * 1024 * 1024)


def like(*shapes):
    return tuple(jax.ShapeDtypeStruct(shape, dtype) for shape, dtype in shapes)


def layer_norm(tokens, offset_row, scale_row):
    average = jnp.mean(tokens, axis=-1, keepdims=True)
    centred = tokens - average
    variance = jnp.mean(centred * centred, axis=-1, keepdims=True)
    return (centred * lax.rsqrt(variance + EPS) * (1.0 + scale_row) + offset_row).astype(
        jnp.bfloat16
    )


def head_norm(values, gain_row):
    power = jnp.mean(values * values, axis=-1, keepdims=True)
    return (values * lax.rsqrt(power + EPS) * gain_row).astype(jnp.bfloat16)


def block_kernel(
    tick, section, patch_flow, own, other, gains, w_qkv, w_out, kv_in, kept, sent, kv, normed, mixed
):
    half, width = own.shape
    rows = 2 * half
    heads = w_out.shape[0] // HS
    here = section[0]
    normed[:half, :] = own[...]
    normed[half:, :] = other[...]
    start = pl.multiple_of(patch_flow[here, tick] * rows, rows)
    kv[...] = kv_in[...]
    gain = gains[here]
    tokens = normed[...]
    keys = dot(tokens, w_qkv[1])
    for head in range(heads):
        part = slice(head * HS, (head + 1) * HS)
        kv[0, pl.ds(start, rows), part] = head_norm(keys[:, part], gain[1:2, :])
    kv[1, pl.ds(start, rows), :] = dot(tokens, w_qkv[2]).astype(jnp.bfloat16)
    queries = dot(tokens, w_qkv[0])
    for head in range(heads):
        part = slice(head * HS, (head + 1) * HS)
        query = head_norm(queries[:, part], gain[0:1, :])
        weights = jnp.exp(dot_rows(query, kv[0, :, part]) / math.sqrt(HS))
        totals = jnp.sum(weights, axis=-1, keepdims=True)
        attended = dot(weights.astype(jnp.bfloat16), kv[1, :, part])
        mixed[:, part] = (attended / totals).astype(jnp.bfloat16)
    tile = width // 4
    heads_out = mixed[...]
    for low in range(0, width, tile):
        projected = dot(heads_out, w_out[:, low : low + tile])
        kept[:, low : low + tile] = projected[:half, :]
        sent[:, low : low + tile] = projected[half:, :].astype(jnp.bfloat16)


def block(tick, section, patch_flow, own, other, gains, w_qkv, w_out, kv):
    half, width = own.shape
    columns = w_out.shape[0]
    return pl.pallas_call(
        functools.partial(block_kernel, tick),
        out_shape=like(
            ((half, width), jnp.float32), ((half, width), jnp.bfloat16), (kv.shape, jnp.bfloat16)
        ),
        in_specs=[SCALARS] * 2 + [WHOLE] * 6,
        out_specs=(WHOLE,) * 3,
        scratch_shapes=[
            VMEM((2 * half, width), jnp.bfloat16),
            VMEM((2 * half, columns), jnp.bfloat16),
        ],
        input_output_aliases={7: 2},
        compiler_params=params(8),
        cost_estimate=pl.CostEstimate(
            flops=16 * half * columns * width,
            bytes_accessed=8 * columns * width,
            transcendentals=0,
        ),
        name="block",
    )(section, patch_flow, own, other, gains, w_qkv, w_out, kv)


def split_kernel(kept, came, mine, *others):
    rows = mine.shape[0]
    mine[...] = kept[:rows, :] + f32(came[:rows, :])
    for place, out in enumerate(others):
        part = slice((place + 1) * rows, (place + 2) * rows)
        out[...] = (kept[part, :] + f32(came[part, :])).astype(jnp.bfloat16)


def split(kept, came):
    shape = (kept.shape[0] // CHIPS, kept.shape[1])
    return pl.pallas_call(
        split_kernel,
        out_shape=like((shape, jnp.float32), *[(shape, jnp.bfloat16)] * (CHIPS - 1)),
        in_specs=[WHOLE] * 2,
        out_specs=(WHOLE,) * CHIPS,
        compiler_params=params(4),
        name="split",
    )(kept, came)


def finish_kernel(
    section, mine, one, two, three, hidden, latent, mod, final_mod, w_final, w_embed, out, renewed
):
    last = mod.shape[1] - 1
    here = section[0]
    total = mine[...] + f32(one[...]) + f32(two[...]) + f32(three[...])
    gate = mod[2, pl.ds(here, 1), :]
    result = (f32(hidden[...]) + gate * total).astype(jnp.bfloat16)

    @pl.when(here == last)
    def _():
        normed = layer_norm(f32(result), final_mod[0:1, :], final_mod[1:2, :])
        velocity = dot_rows(normed, w_final[...])
        fresh = (f32(latent[...]) + velocity).astype(jnp.bfloat16)
        out[...] = dot(fresh, w_embed[...]).astype(jnp.bfloat16)
        renewed[...] = fresh

    @pl.when(here != last)
    def _():
        out[...] = result
        renewed[...] = latent[...]


def finish_packet_kernel(
    section, mine, one, two, three, packet, mod, final_mod, w_final, w_embed, *outs
):
    width, channels = w_embed.shape[1], w_embed.shape[0]
    views = [packet.at[:, :width], packet.at[:, width : width + channels]]
    if len(outs) == 1:
        outs = [outs[0].at[:, :width], outs[0].at[:, width : width + channels]]
    finish_kernel(
        section, mine, one, two, three, *views, mod, final_mod, w_final, w_embed, *outs
    )


def finish_first_kernel(
    section, mine, one, two, three, hidden, latent, mod, final_mod, w_final, w_embed, packet
):
    width, channels = w_embed.shape[1], w_embed.shape[0]
    outs = [packet.at[:, :width], packet.at[:, width : width + channels]]
    finish_kernel(
        section, mine, one, two, three, hidden, latent, mod, final_mod, w_final, w_embed, *outs
    )


def finish(section, parts, state, mod, final_mod, w_final, w_embed, packed):
    rows, width = parts[0].shape
    channels = w_embed.shape[0]
    shapes = [(rows, width + LANES)] if packed else [(rows, width), (rows, channels)]
    args = [*parts, *state, mod, final_mod, w_final, w_embed]
    return pl.pallas_call(
        finish_packet_kernel if len(state) == 1 else finish_first_kernel,
        out_shape=like(*[(shape, jnp.bfloat16) for shape in shapes]),
        in_specs=[SCALARS] + [WHOLE] * len(args),
        out_specs=(WHOLE,) * len(shapes),
        compiler_params=params(4),
        name="finish",
    )(section, *args)


def norm_kernel(section, values, mod, normed):
    here = section[0]
    tokens = f32(values[:, : normed.shape[1]])
    normed[...] = layer_norm(
        tokens, mod[0, pl.ds(here, 1), :], mod[1, pl.ds(here, 1), :]
    )


def norm(section, values, mod):
    return pl.pallas_call(
        norm_kernel,
        out_shape=jax.ShapeDtypeStruct((values.shape[0], mod.shape[2]), jnp.bfloat16),
        in_specs=[SCALARS] + [WHOLE] * 2,
        out_specs=WHOLE,
        compiler_params=params(4),
        name="norm",
    )(section, values, mod)


def exchange(value, apart):
    route = [(device, device ^ apart) for device in range(lax.axis_size("section"))]
    return lax.ppermute(value, "section", route)


def gather_chips(rows):
    return jnp.concatenate([rows] + [exchange(rows, apart) for apart in CHIP_STEPS], 0)


def body(
    hidden_in,
    latent_in,
    w_qkv,
    w_out,
    stale_kv,
    qk_gain,
    block_mod,
    final_mod,
    w_final,
    w_embed,
    patch_flow,
):
    size = lax.axis_size("section")
    ticks = patch_flow.shape[0]
    patch_flow = jnp.transpose(patch_flow)
    section = (lax.axis_index("section") // GROUP).astype(jnp.int32).reshape(1)
    mod = jnp.transpose(block_mod, (1, 0, 2))
    w_final = jnp.transpose(w_final)
    kv = stale_kv
    onward = [(device, (device + GROUP) % size) for device in range(size)]

    state = (hidden_in, latent_in)
    for tick in range(ticks):
        own = gather_chips(norm(section, state[0], mod))
        other = exchange(own, 1)
        kept, sent, kv = block(
            tick, section, patch_flow, own, other, qk_gain, w_qkv, w_out, kv
        )
        mine, *blocks = split(kept, exchange(sent, 1))
        parts = [mine] + [exchange(rows, apart) for rows, apart in zip(blocks, CHIP_STEPS)]
        packed = tick < ticks - 1
        state = finish(section, parts, state, mod, final_mod, w_final, w_embed, packed)
        state = tuple(lax.ppermute(value, "section", onward) for value in state)
    return state


def solution(mesh):
    in_specs = (
        P(("groups", "section"), None),
        P(("groups", "section"), None),
        P(None, None, "section"),
        P("section", None),
        P("groups", None, "section"),
        P(),
        P("groups", None, None),
        P("groups", None),
        P(),
        P(),
        P(),
    )
    out_specs = (P(("groups", "section"), None), P(("groups", "section"), None))
    return jax.shard_map(body, mesh=mesh, in_specs=in_specs, out_specs=out_specs, check_vma=False)
```

```python
import functools
import math

import jax
import jax.numpy as jnp
from jax import lax
from jax.experimental import pallas as pl
from jax.experimental.pallas import tpu as pltpu
from jax.sharding import PartitionSpec as P

HS = 128
GROUP = 8
CHIPS = 4
CHIP_STEPS = (2, 4, 6)
LANES = 128
EPS = 1e-6
VMEM = pltpu.VMEM
WHOLE = pl.BlockSpec(memory_space=pltpu.VMEM)
SCALARS = pl.BlockSpec(memory_space=pltpu.SMEM)


def f32(value):
    return value.astype(jnp.float32)


def dot(left, right):
    return jnp.dot(left, right, preferred_element_type=jnp.float32)


def dot_rows(left, right):
    return lax.dot_general(
        left, right, (((1,), (1,)), ((), ())), preferred_element_type=jnp.float32
    )


def params(mebibytes):
    return pltpu.CompilerParams(vmem_limit_bytes=mebibytes * 1024 * 1024)


def like(*shapes):
    return tuple(jax.ShapeDtypeStruct(shape, dtype) for shape, dtype in shapes)


def layer_norm(tokens, offset_row, scale_row):
    average = jnp.mean(tokens, axis=-1, keepdims=True)
    centred = tokens - average
    variance = jnp.mean(centred * centred, axis=-1, keepdims=True)
    return (centred * lax.rsqrt(variance + EPS) * (1.0 + scale_row) + offset_row).astype(
        jnp.bfloat16
    )


def head_norm(values, gain_row):
    power = jnp.mean(values * values, axis=-1, keepdims=True)
    return (values * lax.rsqrt(power + EPS) * gain_row).astype(jnp.bfloat16)


def block_kernel(
    tick, section, patch_flow, own, other, gains, w_qkv, w_out, kv_in, kept, sent, kv, normed, mixed
):
    half, width = own.shape
    rows = 2 * half
    heads = w_out.shape[0] // HS
    here = section[0]
    normed[:half, :] = own[...]
    normed[half:, :] = other[...]
    start = pl.multiple_of(patch_flow[here, tick] * rows, rows)
    kv[...] = kv_in[...]
    gain = gains[here]
    tokens = normed[...]
    keys = dot(tokens, w_qkv[1])
    for head in range(heads):
        part = slice(head * HS, (head + 1) * HS)
        kv[0, pl.ds(start, rows), part] = head_norm(keys[:, part], gain[1:2, :])
    kv[1, pl.ds(start, rows), :] = dot(tokens, w_qkv[2]).astype(jnp.bfloat16)
    queries = dot(tokens, w_qkv[0])
    for head in range(heads):
        part = slice(head * HS, (head + 1) * HS)
        query = head_norm(queries[:, part], gain[0:1, :])
        weights = jnp.exp(dot_rows(query, kv[0, :, part]) / math.sqrt(HS))
        totals = jnp.sum(weights, axis=-1, keepdims=True)
        attended = dot(weights.astype(jnp.bfloat16), kv[1, :, part])
        mixed[:, part] = (attended / totals).astype(jnp.bfloat16)
    tile = width // 4
    heads_out = mixed[...]
    for low in range(0, width, tile):
        projected = dot(heads_out, w_out[:, low : low + tile])
        kept[:, low : low + tile] = projected[:half, :]
        sent[:, low : low + tile] = projected[half:, :].astype(jnp.bfloat16)


def block(tick, section, patch_flow, own, other, gains, w_qkv, w_out, kv):
    half, width = own.shape
    columns = w_out.shape[0]
    return pl.pallas_call(
        functools.partial(block_kernel, tick),
        out_shape=like(
            ((half, width), jnp.float32), ((half, width), jnp.bfloat16), (kv.shape, jnp.bfloat16)
        ),
        in_specs=[SCALARS] * 2 + [WHOLE] * 6,
        out_specs=(WHOLE,) * 3,
        scratch_shapes=[
            VMEM((2 * half, width), jnp.bfloat16),
            VMEM((2 * half, columns), jnp.bfloat16),
        ],
        input_output_aliases={7: 2},
        compiler_params=params(8),
        cost_estimate=pl.CostEstimate(
            flops=16 * half * columns * width,
            bytes_accessed=8 * columns * width,
            transcendentals=0,
        ),
        name="block",
    )(section, patch_flow, own, other, gains, w_qkv, w_out, kv)


def split_kernel(kept, came, mine, *others):
    rows = mine.shape[0]
    mine[...] = kept[:rows, :] + f32(came[:rows, :])
    for place, out in enumerate(others):
        part = slice((place + 1) * rows, (place + 2) * rows)
        out[...] = (kept[part, :] + f32(came[part, :])).astype(jnp.bfloat16)


def split(kept, came):
    shape = (kept.shape[0] // CHIPS, kept.shape[1])
    return pl.pallas_call(
        split_kernel,
        out_shape=like((shape, jnp.float32), *[(shape, jnp.bfloat16)] * (CHIPS - 1)),
        in_specs=[WHOLE] * 2,
        out_specs=(WHOLE,) * CHIPS,
        compiler_params=params(4),
        name="split",
    )(kept, came)


def finish_kernel(first_tick, *refs):
    (section, mine, one, two, three), refs = refs[:5], refs[5:]
    mod, final_mod, w_final, w_embed, packet = refs[-5:]
    width, channels = w_embed.shape[1], w_embed.shape[0]
    if first_tick:
        hidden, latent = refs[:2]
    else:
        hidden, latent = refs[0].at[:, :width], refs[0].at[:, width : width + channels]
    last = mod.shape[1] - 1
    here = section[0]
    total = mine[...] + f32(one[...]) + f32(two[...]) + f32(three[...])
    gate = mod[2, pl.ds(here, 1), :]
    result = (f32(hidden[...]) + gate * total).astype(jnp.bfloat16)

    @pl.when(here == last)
    def _():
        normed = layer_norm(f32(result), final_mod[0:1, :], final_mod[1:2, :])
        velocity = dot_rows(normed, w_final[...])
        fresh = (f32(latent[...]) + velocity).astype(jnp.bfloat16)
        packet[:, :width] = dot(fresh, w_embed[...]).astype(jnp.bfloat16)
        packet[:, width : width + channels] = fresh

    @pl.when(here != last)
    def _():
        packet[:, :width] = result
        packet[:, width : width + channels] = latent[...]


def finish(section, parts, state, mod, final_mod, w_final, w_embed):
    rows, width = parts[0].shape
    args = [*parts, *state, mod, final_mod, w_final, w_embed]
    return pl.pallas_call(
        functools.partial(finish_kernel, len(state) == 2),
        out_shape=jax.ShapeDtypeStruct((rows, width + LANES), jnp.bfloat16),
        in_specs=[SCALARS] + [WHOLE] * len(args),
        out_specs=WHOLE,
        compiler_params=params(4),
        name="finish",
    )(section, *args)


def norm_kernel(section, values, mod, normed):
    here = section[0]
    tokens = f32(values[:, : normed.shape[1]])
    normed[...] = layer_norm(
        tokens, mod[0, pl.ds(here, 1), :], mod[1, pl.ds(here, 1), :]
    )


def norm(section, values, mod):
    return pl.pallas_call(
        norm_kernel,
        out_shape=jax.ShapeDtypeStruct((values.shape[0], mod.shape[2]), jnp.bfloat16),
        in_specs=[SCALARS] + [WHOLE] * 2,
        out_specs=WHOLE,
        compiler_params=params(4),
        name="norm",
    )(section, values, mod)


def load_kernel(count, *refs):
    sources, targets, semaphores = refs[:count], refs[count : 2 * count], refs[2 * count :]
    copies = [pltpu.make_async_copy(*each) for each in zip(sources, targets, semaphores)]
    for copy in copies:
        copy.start()
    for copy in copies:
        copy.wait()


def load(*arrays):
    count = len(arrays)
    size = sum(array.size * array.dtype.itemsize for array in arrays)
    return pl.pallas_call(
        functools.partial(load_kernel, count),
        out_shape=tuple(pltpu.VMEM(array.shape, array.dtype) for array in arrays),
        in_specs=[pl.BlockSpec(memory_space=pltpu.HBM)] * count,
        out_specs=(WHOLE,) * count,
        scratch_shapes=[pltpu.SemaphoreType.DMA(())] * count,
        compiler_params=params(60 - -(-size >> 20)),
        cost_estimate=pl.CostEstimate(flops=0, bytes_accessed=2 * size, transcendentals=0),
        name="load",
    )(*arrays)


def first_kernel(section, hidden_in, mod_in, hidden, mod, normed, one, two):
    copies = [
        pltpu.make_async_copy(hidden_in, hidden, one),
        pltpu.make_async_copy(mod_in, mod, two),
    ]
    for copy in copies:
        copy.start()
    for copy in copies:
        copy.wait()
    norm_kernel(section, hidden, mod, normed)


def first(section, hidden, mod):
    far = pl.BlockSpec(memory_space=pltpu.HBM)
    return pl.pallas_call(
        first_kernel,
        out_shape=(
            VMEM(hidden.shape, hidden.dtype),
            VMEM(mod.shape, mod.dtype),
            jax.ShapeDtypeStruct(hidden.shape, jnp.bfloat16),
        ),
        in_specs=[SCALARS, far, far],
        out_specs=(WHOLE,) * 3,
        scratch_shapes=[pltpu.SemaphoreType.DMA(())] * 2,
        compiler_params=params(60),
        name="first",
    )(section, hidden, mod)


def open_kernel(packet, hidden, latent):
    width = hidden.shape[1]
    hidden[...] = packet[:, :width]
    latent[...] = packet[:, width : width + latent.shape[1]]


def open_packet(packet, width, channels):
    return pl.pallas_call(
        open_kernel,
        out_shape=like(
            ((packet.shape[0], width), jnp.bfloat16), ((packet.shape[0], channels), jnp.bfloat16)
        ),
        in_specs=[WHOLE],
        out_specs=(WHOLE,) * 2,
        compiler_params=params(4),
        name="open",
    )(packet)


def exchange(value, apart):
    route = [(device, device ^ apart) for device in range(lax.axis_size("section"))]
    return lax.ppermute(value, "section", route)


def gather_chips(rows):
    return jnp.concatenate([rows] + [exchange(rows, apart) for apart in CHIP_STEPS], 0)


def body(
    hidden_in,
    latent_in,
    w_qkv,
    w_out,
    stale_kv,
    qk_gain,
    block_mod,
    final_mod,
    w_final,
    w_embed,
    patch_flow,
):
    size = lax.axis_size("section")
    ticks = patch_flow.shape[0]
    section = (lax.axis_index("section") // GROUP).astype(jnp.int32).reshape(1)
    width, channels = hidden_in.shape[1], latent_in.shape[1]
    w_final = jnp.transpose(w_final)
    onward = [(device, (device + GROUP) % size) for device in range(size)]

    hidden, mod, normed = first(section, hidden_in, jnp.transpose(block_mod, (1, 0, 2)))
    held = (w_qkv, w_out, qk_gain, jnp.transpose(patch_flow), stale_kv)
    normed, *held = lax.optimization_barrier((normed, *held))
    held = load(*held)
    state = (hidden, latent_in)
    for tick in range(ticks):
        if tick > 0:
            normed = norm(section, state[0], mod)
        own = gather_chips(normed)
        if tick == 0:
            own, w_qkv, w_out, gains, patch_flow, kv = lax.optimization_barrier((own, *held))
        other = exchange(own, 1)
        kept, sent, kv = block(tick, section, patch_flow, own, other, gains, w_qkv, w_out, kv)
        mine, *blocks = split(kept, exchange(sent, 1))
        came = [exchange(rows, apart) for rows, apart in zip(blocks, CHIP_STEPS)]
        parts = [mine] + came[::-1]
        packet = finish(section, parts, state, mod, final_mod, w_final, w_embed)
        state = (lax.ppermute(packet, "section", onward),)
    return open_packet(state[0], width, channels)


def solution(mesh):
    in_specs = (
        P(("groups", "section"), None),
        P(("groups", "section"), None),
        P(None, None, "section"),
        P("section", None),
        P("groups", None, "section"),
        P(),
        P("groups", None, None),
        P("groups", None),
        P(),
        P(),
        P(),
    )
    out_specs = (P(("groups", "section"), None), P(("groups", "section"), None))
    return jax.shard_map(body, mesh=mesh, in_specs=in_specs, out_specs=out_specs, check_vma=False)
```

```python
import functools
import math

import jax
import jax.numpy as jnp
from jax import lax
from jax.experimental import pallas as pl
from jax.experimental.pallas import tpu as pltpu
from jax.sharding import PartitionSpec as P

HS = 128
GROUP = 8
CHIPS = 4
CHIP_STEPS = (2, 4, 6)
LANES = 128
EPS = 1e-6
VMEM = pltpu.VMEM
WHOLE = pl.BlockSpec(memory_space=pltpu.VMEM)
SCALARS = pl.BlockSpec(memory_space=pltpu.SMEM)


def f32(value):
    return value.astype(jnp.float32)


def dot(left, right):
    return jnp.dot(left, right, preferred_element_type=jnp.float32)


def dot_rows(left, right):
    return lax.dot_general(
        left, right, (((1,), (1,)), ((), ())), preferred_element_type=jnp.float32
    )


def params(mebibytes):
    return pltpu.CompilerParams(vmem_limit_bytes=mebibytes * 1024 * 1024)


def like(*shapes):
    return tuple(jax.ShapeDtypeStruct(shape, dtype) for shape, dtype in shapes)


def layer_norm(tokens, offset_row, scale_row):
    average = jnp.mean(tokens, axis=-1, keepdims=True)
    centred = tokens - average
    variance = jnp.mean(centred * centred, axis=-1, keepdims=True)
    return (centred * lax.rsqrt(variance + EPS) * (1.0 + scale_row) + offset_row).astype(
        jnp.bfloat16
    )


def head_norm(values, gain_row):
    power = jnp.mean(values * values, axis=-1, keepdims=True)
    return (values * lax.rsqrt(power + EPS) * gain_row).astype(jnp.bfloat16)


def block_kernel(
    tick, section, patch_flow, *refs
):
    pieces, refs = refs[: 2 * CHIPS], refs[2 * CHIPS :]
    gains, w_qkv, w_out, kv_in, kept, sent, ahead, kv, normed, mixed = refs
    part_rows, width = pieces[0].shape
    half = CHIPS * part_rows
    rows = 2 * half
    heads = w_out.shape[0] // HS
    here = section[0]
    for place, piece in enumerate(pieces):
        normed[place * part_rows : (place + 1) * part_rows, :] = piece[...]
    start = pl.multiple_of(patch_flow[here, tick] * rows, rows)
    kv[...] = kv_in[...]
    gain = gains[here]
    tokens = normed[...]
    columns = w_out.shape[0]
    products = dot(tokens, w_qkv[...])
    queries, keys = products[:, :columns], products[:, columns : 2 * columns]
    for head in range(heads):
        part = slice(head * HS, (head + 1) * HS)
        kv[0, pl.ds(start, rows), part] = head_norm(keys[:, part], gain[1:2, :])
    kv[1, pl.ds(start, rows), :] = products[:, 2 * columns :].astype(jnp.bfloat16)
    for head in range(heads):
        part = slice(head * HS, (head + 1) * HS)
        query = head_norm(queries[:, part], gain[0:1, :])
        weights = jnp.exp(dot_rows(query, kv[0, :, part]) / math.sqrt(HS))
        totals = jnp.sum(weights, axis=-1, keepdims=True)
        attended = dot(weights.astype(jnp.bfloat16), kv[1, :, part])
        mixed[:, part] = (attended / totals).astype(jnp.bfloat16)
    tile = width // 4
    heads_out = mixed[...]
    edge = rows - half // CHIPS
    for low in range(0, width, tile):
        projected = dot(heads_out, w_out[:, low : low + tile])
        kept[:, low : low + tile] = projected[:half, :]
        sent[:, low : low + tile] = projected[half:edge, :].astype(jnp.bfloat16)
        ahead[:, low : low + tile] = projected[edge:, :].astype(jnp.bfloat16)


def block(tick, section, patch_flow, pieces, gains, w_qkv, w_out, kv):
    half, width = CHIPS * pieces[0].shape[0], pieces[0].shape[1]
    columns = w_out.shape[0]
    return pl.pallas_call(
        functools.partial(block_kernel, tick),
        out_shape=like(
            ((half, width), jnp.float32),
            ((half - half // CHIPS, width), jnp.bfloat16),
            ((half // CHIPS, width), jnp.bfloat16),
            (kv.shape, jnp.bfloat16),
        ),
        in_specs=[SCALARS] * 2 + [WHOLE] * (4 + 2 * CHIPS),
        out_specs=(WHOLE,) * 4,
        scratch_shapes=[
            VMEM((2 * half, width), jnp.bfloat16),
            VMEM((2 * half, columns), jnp.bfloat16),
        ],
        input_output_aliases={5 + 2 * CHIPS: 3},
        compiler_params=params(8),
        cost_estimate=pl.CostEstimate(
            flops=16 * half * columns * width,
            bytes_accessed=8 * columns * width,
            transcendentals=0,
        ),
        name="block",
    )(section, patch_flow, *pieces, gains, w_qkv, w_out, kv)


def split_last_kernel(kept, came, out):
    rows = out.shape[0]
    out[...] = (kept[-rows:, :] + f32(came[...])).astype(jnp.bfloat16)


def split_last(kept, came):
    return pl.pallas_call(
        split_last_kernel,
        out_shape=jax.ShapeDtypeStruct(came.shape, jnp.bfloat16),
        in_specs=[WHOLE] * 2,
        out_specs=WHOLE,
        compiler_params=params(4),
        name="split_last",
    )(kept, came)


def split_kernel(kept, came, mine, *others):
    rows = mine.shape[0]
    mine[...] = kept[:rows, :] + f32(came[:rows, :])
    for place, out in enumerate(others):
        part = slice((place + 1) * rows, (place + 2) * rows)
        out[...] = (kept[part, :] + f32(came[part, :])).astype(jnp.bfloat16)


def split(kept, came):
    shape = (kept.shape[0] // CHIPS, kept.shape[1])
    return pl.pallas_call(
        split_kernel,
        out_shape=like((shape, jnp.float32), *[(shape, jnp.bfloat16)] * (CHIPS - 2)),
        in_specs=[WHOLE] * 2,
        out_specs=(WHOLE,) * (CHIPS - 1),
        compiler_params=params(4),
        name="split",
    )(kept, came)


def finish_kernel(first_tick, *refs):
    (section, mine, one, two, three), refs = refs[:5], refs[5:]
    mod, final_mod, w_final, w_embed, packet = refs[-5:]
    width, channels = w_embed.shape[1], w_embed.shape[0]
    hidden, latent = refs[:2]
    if not first_tick:
        latent = latent.at[:, width : width + channels]
    last = mod.shape[1] - 1
    here = section[0]
    total = mine[...] + f32(one[...]) + f32(two[...]) + f32(three[...])
    gate = mod[2, pl.ds(here, 1), :]
    result = (f32(hidden[...]) + gate * total).astype(jnp.bfloat16)

    @pl.when(here == last)
    def _():
        normed = layer_norm(f32(result), final_mod[0:1, :], final_mod[1:2, :])
        velocity = dot_rows(normed, w_final[...])
        fresh = (f32(latent[...]) + velocity).astype(jnp.bfloat16)
        packet[:, width : width + channels] = fresh

    @pl.when(here != last)
    def _():
        packet[:, :width] = result
        packet[:, width : width + channels] = latent[...]


def finish(section, parts, state, mod, final_mod, w_final, w_embed):
    rows, width = parts[0].shape
    args = [*parts, *state, mod, final_mod, w_final, w_embed]
    return pl.pallas_call(
        functools.partial(finish_kernel, state[1].shape[1] == w_embed.shape[0]),
        out_shape=jax.ShapeDtypeStruct((rows, width + LANES), jnp.bfloat16),
        in_specs=[SCALARS] + [WHOLE] * len(args),
        out_specs=WHOLE,
        compiler_params=params(4),
        name="finish",
    )(section, *args)


def norm_here(section, tokens, mod):
    here = section[0]
    return layer_norm(tokens, mod[0, pl.ds(here, 1), :], mod[1, pl.ds(here, 1), :])


def arrive(section, packet, w_embed, hidden):
    width, channels = w_embed.shape[1], w_embed.shape[0]

    @pl.when(section[0] == 0)
    def _():
        latent = packet[:, width : width + channels]
        hidden[...] = dot(latent, w_embed[...]).astype(jnp.bfloat16)

    @pl.when(section[0] != 0)
    def _():
        hidden[...] = packet[:, :width]


def norm_kernel(section, packet, mod, w_embed, hidden, normed):
    arrive(section, packet, w_embed, hidden)
    normed[...] = norm_here(section, f32(hidden[...]), mod)


def norm(section, packet, mod, w_embed):
    shape = ((packet.shape[0], mod.shape[2]), jnp.bfloat16)
    return pl.pallas_call(
        norm_kernel,
        out_shape=like(shape, shape),
        in_specs=[SCALARS] + [WHOLE] * 3,
        out_specs=(WHOLE,) * 2,
        compiler_params=params(4),
        name="norm",
    )(section, packet, mod, w_embed)


def load_kernel(count, *refs):
    sources, targets, semaphores = refs[:count], refs[count : 2 * count], refs[2 * count :]
    parts, _, columns = sources[0].shape
    copies = [
        pltpu.make_async_copy(
            sources[0].at[part],
            targets[0].at[:, part * columns : (part + 1) * columns],
            semaphores[count + part],
        )
        for part in range(parts)
    ]
    rest = zip(sources[1:], targets[1:], semaphores[1:count])
    copies += [pltpu.make_async_copy(*each) for each in rest]
    for copy in copies:
        copy.start()
    for copy in copies:
        copy.wait()


def load(*arrays):
    count = len(arrays)
    parts, depth, columns = arrays[0].shape
    shapes = [(depth, parts * columns)] + [array.shape for array in arrays[1:]]
    size = sum(array.size * array.dtype.itemsize for array in arrays)
    return pl.pallas_call(
        functools.partial(load_kernel, count),
        out_shape=tuple(VMEM(shape, array.dtype) for shape, array in zip(shapes, arrays)),
        in_specs=[pl.BlockSpec(memory_space=pltpu.HBM)] * count,
        out_specs=(WHOLE,) * count,
        scratch_shapes=[pltpu.SemaphoreType.DMA(())] * (count + parts),
        compiler_params=params(60 - -(-size >> 20)),
        cost_estimate=pl.CostEstimate(flops=0, bytes_accessed=2 * size, transcendentals=0),
        name="load",
    )(*arrays)


def first_kernel(section, hidden_in, mod_in, hidden, mod, normed, one, two):
    copies = [
        pltpu.make_async_copy(hidden_in, hidden, one),
        pltpu.make_async_copy(mod_in, mod, two),
    ]
    for copy in copies:
        copy.start()
    for copy in copies:
        copy.wait()
    normed[...] = norm_here(section, f32(hidden[...]), mod)


def first(section, hidden, mod):
    far = pl.BlockSpec(memory_space=pltpu.HBM)
    return pl.pallas_call(
        first_kernel,
        out_shape=(
            VMEM(hidden.shape, hidden.dtype),
            VMEM(mod.shape, mod.dtype),
            jax.ShapeDtypeStruct(hidden.shape, jnp.bfloat16),
        ),
        in_specs=[SCALARS, far, far],
        out_specs=(WHOLE,) * 3,
        scratch_shapes=[pltpu.SemaphoreType.DMA(())] * 2,
        compiler_params=params(60),
        name="first",
    )(section, hidden, mod)


def open_kernel(section, packet, w_embed, hidden, latent):
    width = hidden.shape[1]
    arrive(section, packet, w_embed, hidden)
    latent[...] = packet[:, width : width + latent.shape[1]]


def open_packet(section, packet, w_embed):
    channels, width = w_embed.shape
    return pl.pallas_call(
        open_kernel,
        out_shape=like(
            ((packet.shape[0], width), jnp.bfloat16), ((packet.shape[0], channels), jnp.bfloat16)
        ),
        in_specs=[SCALARS] + [WHOLE] * 2,
        out_specs=(WHOLE,) * 2,
        compiler_params=params(4),
        name="open",
    )(section, packet, w_embed)


def exchange(value, apart):
    route = [(device, device ^ apart) for device in range(lax.axis_size("section"))]
    return lax.ppermute(value, "section", route)


def gather_chips(rows):
    return [rows] + [exchange(rows, apart) for apart in CHIP_STEPS]


def body(
    hidden_in,
    latent_in,
    w_qkv,
    w_out,
    stale_kv,
    qk_gain,
    block_mod,
    final_mod,
    w_final,
    w_embed,
    patch_flow,
):
    size = lax.axis_size("section")
    ticks = patch_flow.shape[0]
    section = (lax.axis_index("section") // GROUP).astype(jnp.int32).reshape(1)
    w_final = jnp.transpose(w_final)
    onward = [(device, (device + GROUP) % size) for device in range(size)]

    hidden, mod, normed = first(section, hidden_in, jnp.transpose(block_mod, (1, 0, 2)))
    held = (w_qkv, w_out, qk_gain, jnp.transpose(patch_flow), stale_kv)
    normed, *held = lax.optimization_barrier((normed, *held))
    held = load(*held)
    state = (hidden, latent_in)
    for tick in range(ticks):
        if tick > 0:
            hidden, normed = norm(section, packet, mod, w_embed)
            state = (hidden, packet)
        own = gather_chips(normed)
        if tick == 0:
            own, w_qkv, w_out, gains, patch_flow, kv = lax.optimization_barrier((own, *held))
        pieces = own + [exchange(piece, 1) for piece in own]
        kept, sent, ahead, kv = block(tick, section, patch_flow, pieces, gains, w_qkv, w_out, kv)
        ahead = split_last(kept, exchange(ahead, 1))
        mine, *blocks = split(kept, exchange(sent, 1))
        came = [exchange(rows, apart) for rows, apart in zip([*blocks, ahead], CHIP_STEPS)]
        parts = [mine] + came[::-1]
        packet = finish(section, parts, state, mod, final_mod, w_final, w_embed)
        packet = lax.ppermute(packet, "section", onward)
    return open_packet(section, packet, w_embed)


def solution(mesh):
    in_specs = (
        P(("groups", "section"), None),
        P(("groups", "section"), None),
        P(None, None, "section"),
        P("section", None),
        P("groups", None, "section"),
        P(),
        P("groups", None, None),
        P("groups", None),
        P(),
        P(),
        P(),
    )
    out_specs = (P(("groups", "section"), None), P(("groups", "section"), None))
    return jax.shard_map(body, mesh=mesh, in_specs=in_specs, out_specs=out_specs, check_vma=False)
```

```python
import functools
import math

import jax
import jax.numpy as jnp
from jax import lax
from jax.experimental import pallas as pl
from jax.experimental.pallas import tpu as pltpu
from jax.sharding import PartitionSpec as P

HS = 128
GROUP = 8
CHIPS = 4
CHIP_STEPS = (2, 4, 6)
LANES = 128
EPS = 1e-6
VMEM = pltpu.VMEM
WHOLE = pl.BlockSpec(memory_space=pltpu.VMEM)
SCALARS = pl.BlockSpec(memory_space=pltpu.SMEM)


def f32(value):
    return value.astype(jnp.float32)


def dot(left, right):
    return jnp.dot(left, right, preferred_element_type=jnp.float32)


def dot_rows(left, right):
    return lax.dot_general(
        left, right, (((1,), (1,)), ((), ())), preferred_element_type=jnp.float32
    )


def params(mebibytes):
    return pltpu.CompilerParams(vmem_limit_bytes=mebibytes * 1024 * 1024)


def like(*shapes):
    return tuple(jax.ShapeDtypeStruct(shape, dtype) for shape, dtype in shapes)


def layer_norm(tokens, offset_row, scale_row):
    average = jnp.mean(tokens, axis=-1, keepdims=True)
    centred = tokens - average
    variance = jnp.mean(centred * centred, axis=-1, keepdims=True)
    return (centred * lax.rsqrt(variance + EPS) * (1.0 + scale_row) + offset_row).astype(
        jnp.bfloat16
    )


def head_norm(values, gain_row):
    power = jnp.mean(values * values, axis=-1, keepdims=True)
    return (values * lax.rsqrt(power + EPS) * gain_row).astype(jnp.bfloat16)


def norm_here(section, tokens, mod):
    here = section[0]
    return layer_norm(tokens, mod[0, pl.ds(here, 1), :], mod[1, pl.ds(here, 1), :])


def block_kernel(tick, section, patch_flow, *refs):
    pieces, refs = refs[: 2 * CHIPS], refs[2 * CHIPS :]
    if tick == 0:
        mod, refs = refs[0], refs[1:]
    gains, w_qkv, w_out, kv_in, kept, sent, ahead, kv, normed, mixed = refs
    part_rows, width = pieces[0].shape
    half = CHIPS * part_rows
    rows = 2 * half
    heads = w_out.shape[0] // HS
    here = section[0]
    for place, piece in enumerate(pieces):
        values = piece[...]
        if tick == 0:
            values = norm_here(section, f32(values), mod)
        normed[place * part_rows : (place + 1) * part_rows, :] = values
    start = pl.multiple_of(patch_flow[here, tick] * rows, rows)
    kv[...] = kv_in[...]
    gain = gains[here]
    tokens = normed[...]
    columns = w_out.shape[0]
    products = dot(tokens, w_qkv[...])
    queries, keys = products[:, :columns], products[:, columns : 2 * columns]
    for head in range(heads):
        part = slice(head * HS, (head + 1) * HS)
        kv[0, pl.ds(start, rows), part] = head_norm(keys[:, part], gain[1:2, :])
    kv[1, pl.ds(start, rows), :] = products[:, 2 * columns :].astype(jnp.bfloat16)
    for head in range(heads):
        part = slice(head * HS, (head + 1) * HS)
        query = head_norm(queries[:, part], gain[0:1, :])
        weights = jnp.exp(dot_rows(query, kv[0, :, part]) / math.sqrt(HS))
        totals = jnp.sum(weights, axis=-1, keepdims=True)
        attended = dot(weights.astype(jnp.bfloat16), kv[1, :, part])
        mixed[:, part] = (attended / totals).astype(jnp.bfloat16)
    tile = width // 4
    heads_out = mixed[...]
    edge = rows - half // CHIPS
    for low in range(0, width, tile):
        projected = dot(heads_out, w_out[:, low : low + tile])
        kept[:, low : low + tile] = projected[:half, :]
        sent[:, low : low + tile] = projected[half:edge, :].astype(jnp.bfloat16)
        ahead[:, low : low + tile] = projected[edge:, :].astype(jnp.bfloat16)


def block(tick, section, patch_flow, pieces, mod, gains, w_qkv, w_out, kv):
    half, width = CHIPS * pieces[0].shape[0], pieces[0].shape[1]
    columns = w_out.shape[0]
    args = [section, patch_flow, *pieces] + [mod] * (tick == 0) + [gains, w_qkv, w_out, kv]
    return pl.pallas_call(
        functools.partial(block_kernel, tick),
        out_shape=like(
            ((half, width), jnp.float32),
            ((half - half // CHIPS, width), jnp.bfloat16),
            ((half // CHIPS, width), jnp.bfloat16),
            (kv.shape, jnp.bfloat16),
        ),
        in_specs=[SCALARS] * 2 + [WHOLE] * (len(args) - 2),
        out_specs=(WHOLE,) * 4,
        scratch_shapes=[
            VMEM((2 * half, width), jnp.bfloat16),
            VMEM((2 * half, columns), jnp.bfloat16),
        ],
        input_output_aliases={len(args) - 1: 3},
        compiler_params=params(8),
        cost_estimate=pl.CostEstimate(
            flops=16 * half * columns * width,
            bytes_accessed=8 * columns * width,
            transcendentals=0,
        ),
        name="block",
    )(*args)


def split_last_kernel(kept, came, out):
    rows = out.shape[0]
    out[...] = (kept[-rows:, :] + f32(came[...])).astype(jnp.bfloat16)


def split_last(kept, came):
    return pl.pallas_call(
        split_last_kernel,
        out_shape=jax.ShapeDtypeStruct(came.shape, jnp.bfloat16),
        in_specs=[WHOLE] * 2,
        out_specs=WHOLE,
        compiler_params=params(4),
        name="split_last",
    )(kept, came)


def split_kernel(kept, came, mine, *others):
    rows = mine.shape[0]
    mine[...] = kept[:rows, :] + f32(came[:rows, :])
    for place, out in enumerate(others):
        part = slice((place + 1) * rows, (place + 2) * rows)
        out[...] = (kept[part, :] + f32(came[part, :])).astype(jnp.bfloat16)


def split(kept, came):
    shape = (kept.shape[0] // CHIPS, kept.shape[1])
    return pl.pallas_call(
        split_kernel,
        out_shape=like((shape, jnp.float32), *[(shape, jnp.bfloat16)] * (CHIPS - 2)),
        in_specs=[WHOLE] * 2,
        out_specs=(WHOLE,) * (CHIPS - 1),
        compiler_params=params(4),
        name="split",
    )(kept, came)


def finish_kernel(first_tick, *refs):
    (section, mine, one, two, three), refs = refs[:5], refs[5:]
    mod, final_mod, w_final, w_embed, packet = refs[-5:]
    width, channels = w_embed.shape[1], w_embed.shape[0]
    hidden, latent = refs[:2]
    if not first_tick:
        latent = latent.at[:, width : width + channels]
    last = mod.shape[1] - 1
    here = section[0]
    total = mine[...] + f32(one[...]) + f32(two[...]) + f32(three[...])
    gate = mod[2, pl.ds(here, 1), :]
    result = (f32(hidden[...]) + gate * total).astype(jnp.bfloat16)

    @pl.when(here == last)
    def _():
        normed = layer_norm(f32(result), final_mod[0:1, :], final_mod[1:2, :])
        velocity = dot_rows(normed, w_final[...])
        fresh = (f32(latent[...]) + velocity).astype(jnp.bfloat16)
        packet[:, width : width + channels] = fresh

    @pl.when(here != last)
    def _():
        packet[:, :width] = result
        packet[:, width : width + channels] = latent[...]


def finish(section, parts, state, mod, final_mod, w_final, w_embed):
    rows, width = parts[0].shape
    args = [*parts, *state, mod, final_mod, w_final, w_embed]
    return pl.pallas_call(
        functools.partial(finish_kernel, state[1].shape[1] == w_embed.shape[0]),
        out_shape=jax.ShapeDtypeStruct((rows, width + LANES), jnp.bfloat16),
        in_specs=[SCALARS] + [WHOLE] * len(args),
        out_specs=WHOLE,
        compiler_params=params(4),
        name="finish",
    )(section, *args)


def arrive(section, packet, w_embed, hidden):
    width, channels = w_embed.shape[1], w_embed.shape[0]

    @pl.when(section[0] == 0)
    def _():
        latent = packet[:, width : width + channels]
        hidden[...] = dot(latent, w_embed[...]).astype(jnp.bfloat16)

    @pl.when(section[0] != 0)
    def _():
        hidden[...] = packet[:, :width]


def norm_kernel(section, packet, mod, w_embed, hidden, normed):
    arrive(section, packet, w_embed, hidden)
    normed[...] = norm_here(section, f32(hidden[...]), mod)


def norm(section, packet, mod, w_embed):
    shape = ((packet.shape[0], mod.shape[2]), jnp.bfloat16)
    return pl.pallas_call(
        norm_kernel,
        out_shape=like(shape, shape),
        in_specs=[SCALARS] + [WHOLE] * 3,
        out_specs=(WHOLE,) * 2,
        compiler_params=params(4),
        name="norm",
    )(section, packet, mod, w_embed)


def load_kernel(count, *refs):
    sources, targets, semaphores = refs[:count], refs[count : 2 * count], refs[2 * count :]
    parts, _, columns = sources[0].shape
    copies = [
        pltpu.make_async_copy(
            sources[0].at[part],
            targets[0].at[:, part * columns : (part + 1) * columns],
            semaphores[count + part],
        )
        for part in range(parts)
    ]
    rest = zip(sources[1:], targets[1:], semaphores[1:count])
    copies += [pltpu.make_async_copy(*each) for each in rest]
    for copy in copies:
        copy.start()
    for copy in copies:
        copy.wait()


def load(*arrays):
    count = len(arrays)
    parts, depth, columns = arrays[0].shape
    shapes = [(depth, parts * columns)] + [array.shape for array in arrays[1:]]
    size = sum(array.size * array.dtype.itemsize for array in arrays)
    return pl.pallas_call(
        functools.partial(load_kernel, count),
        out_shape=tuple(VMEM(shape, array.dtype) for shape, array in zip(shapes, arrays)),
        in_specs=[pl.BlockSpec(memory_space=pltpu.HBM)] * count,
        out_specs=(WHOLE,) * count,
        scratch_shapes=[pltpu.SemaphoreType.DMA(())] * (count + parts),
        compiler_params=params(60 - -(-size >> 20)),
        cost_estimate=pl.CostEstimate(flops=0, bytes_accessed=2 * size, transcendentals=0),
        name="load",
    )(*arrays)


def open_kernel(section, packet, w_embed, hidden, latent):
    width = hidden.shape[1]
    arrive(section, packet, w_embed, hidden)
    latent[...] = packet[:, width : width + latent.shape[1]]


def open_packet(section, packet, w_embed):
    channels, width = w_embed.shape
    return pl.pallas_call(
        open_kernel,
        out_shape=like(
            ((packet.shape[0], width), jnp.bfloat16), ((packet.shape[0], channels), jnp.bfloat16)
        ),
        in_specs=[SCALARS] + [WHOLE] * 2,
        out_specs=(WHOLE,) * 2,
        compiler_params=params(4),
        name="open",
    )(section, packet, w_embed)


def exchange(value, apart):
    route = [(device, device ^ apart) for device in range(lax.axis_size("section"))]
    return lax.ppermute(value, "section", route)


def gather_chips(rows):
    return [rows] + [exchange(rows, apart) for apart in CHIP_STEPS]


def body(
    hidden_in,
    latent_in,
    w_qkv,
    w_out,
    stale_kv,
    qk_gain,
    block_mod,
    final_mod,
    w_final,
    w_embed,
    patch_flow,
):
    size = lax.axis_size("section")
    ticks = patch_flow.shape[0]
    section = (lax.axis_index("section") // GROUP).astype(jnp.int32).reshape(1)
    w_final = jnp.transpose(w_final)
    onward = [(device, (device + GROUP) % size) for device in range(size)]
    across = [(device, target ^ (GROUP // 2)) for device, target in onward]

    mod = jnp.transpose(block_mod, (1, 0, 2))
    held = load(w_qkv, w_out, qk_gain, jnp.transpose(patch_flow), stale_kv, mod)
    section, normed = lax.optimization_barrier((section, hidden_in))
    state = (hidden_in, latent_in)
    for tick in range(ticks):
        if tick > 0:
            hidden, normed = norm(section, packet, mod, w_embed)
            state = (hidden, packet)
        own = gather_chips(normed)
        if tick == 0:
            own, w_qkv, w_out, gains, patch_flow, kv, mod = lax.optimization_barrier((own, *held))
        pieces = own + [exchange(piece, 1) for piece in own]
        kept, sent, ahead, kv = block(tick, section, patch_flow, pieces, mod, gains, w_qkv, w_out, kv)
        ahead = split_last(kept, exchange(ahead, 1))
        mine, *blocks = split(kept, exchange(sent, 1))
        came = [exchange(rows, apart) for rows, apart in zip([*blocks, ahead], CHIP_STEPS)]
        parts = [mine] + came[::-1]
        packet = finish(section, parts, state, mod, final_mod, w_final, w_embed)
        swaps = tick < ticks - ticks % 2
        packet = lax.ppermute(packet, "section", across if swaps else onward)
    return open_packet(section, packet, w_embed)


def solution(mesh):
    in_specs = (
        P(("groups", "section"), None),
        P(("groups", "section"), None),
        P(None, None, "section"),
        P("section", None),
        P("groups", None, "section"),
        P(),
        P("groups", None, None),
        P("groups", None),
        P(),
        P(),
        P(),
    )
    out_specs = (P(("groups", "section"), None), P(("groups", "section"), None))
    return jax.shard_map(body, mesh=mesh, in_specs=in_specs, out_specs=out_specs, check_vma=False)
```

```python
import functools
import math

import jax
import jax.numpy as jnp
from jax import lax
from jax.experimental import pallas as pl
from jax.experimental.pallas import tpu as pltpu
from jax.sharding import PartitionSpec as P


HS = 128
GROUP = 8
CHIPS = 4
CHIP_STEPS = (2, 4, 6)
LANES = 128
EPS = 1e-6
VMEM = pltpu.VMEM
WHOLE = pl.BlockSpec(memory_space=pltpu.VMEM)
SCALARS = pl.BlockSpec(memory_space=pltpu.SMEM)


def f32(value):
    return value.astype(jnp.float32)


def dot(left, right):
    return jnp.dot(left, right, preferred_element_type=jnp.float32)


def dot_rows(left, right):
    return lax.dot_general(
        left, right, (((1,), (1,)), ((), ())), preferred_element_type=jnp.float32
    )


def params(mebibytes):
    return pltpu.CompilerParams(vmem_limit_bytes=mebibytes * 1024 * 1024)


def like(*shapes):
    return tuple(jax.ShapeDtypeStruct(shape, dtype) for shape, dtype in shapes)


def layer_norm(tokens, offset_row, scale_row):
    average = jnp.mean(tokens, axis=-1, keepdims=True)
    centred = tokens - average
    variance = jnp.mean(centred * centred, axis=-1, keepdims=True)
    return (centred * lax.rsqrt(variance + EPS) * (1.0 + scale_row) + offset_row).astype(
        jnp.bfloat16
    )


def head_norm(values, gain_row):
    power = jnp.mean(values * values, axis=-1, keepdims=True)
    return (values * lax.rsqrt(power + EPS) * gain_row).astype(jnp.bfloat16)


def norm_here(section, tokens, mod):
    here = section[0]
    return layer_norm(tokens, mod[0, pl.ds(here, 1), :], mod[1, pl.ds(here, 1), :])


def block_kernel(tick, section, patch_flow, *refs):
    pieces, refs = refs[: 2 * CHIPS], refs[2 * CHIPS :]
    if tick == 0:
        mod, refs = refs[0], refs[1:]
    gains, w_qkv, w_out, kv_in, kept, sent, ahead, kv, normed, mixed = refs
    part_rows, width = pieces[0].shape
    half = CHIPS * part_rows
    rows = 2 * half
    heads = w_out.shape[0] // HS
    here = section[0]
    for place, piece in enumerate(pieces):
        values = piece[...]
        if tick == 0:
            values = norm_here(section, f32(values), mod)
        normed[place * part_rows : (place + 1) * part_rows, :] = values
    start = pl.multiple_of(patch_flow[here, tick] * rows, rows)
    kv[...] = kv_in[...]
    gain = gains[here]
    tokens = normed[...]
    columns = w_out.shape[0]
    products = dot(tokens, w_qkv[...])
    queries, keys = products[:, :columns], products[:, columns : 2 * columns]
    for head in range(heads):
        part = slice(head * HS, (head + 1) * HS)
        kv[0, pl.ds(start, rows), part] = head_norm(keys[:, part], gain[1:2, :])
    kv[1, pl.ds(start, rows), :] = products[:, 2 * columns :].astype(jnp.bfloat16)
    for head in range(heads):
        part = slice(head * HS, (head + 1) * HS)
        query = head_norm(queries[:, part], gain[0:1, :])
        weights = jnp.exp(dot_rows(query, kv[0, :, part]) / math.sqrt(HS))
        totals = jnp.sum(weights, axis=-1, keepdims=True)
        attended = dot(weights.astype(jnp.bfloat16), kv[1, :, part])
        mixed[:, part] = (attended / totals).astype(jnp.bfloat16)
    tile = width // 4
    heads_out = mixed[...]
    edge = rows - half // CHIPS
    for low in range(0, width, tile):
        projected = dot(heads_out, w_out[:, low : low + tile])
        kept[:, low : low + tile] = projected[:half, :]
        sent[:, low : low + tile] = projected[half:edge, :].astype(jnp.bfloat16)
        ahead[:, low : low + tile] = projected[edge:, :].astype(jnp.bfloat16)


def block(tick, section, patch_flow, pieces, mod, gains, w_qkv, w_out, kv):
    half, width = CHIPS * pieces[0].shape[0], pieces[0].shape[1]
    columns = w_out.shape[0]
    args = [section, patch_flow, *pieces] + [mod] * (tick == 0) + [gains, w_qkv, w_out, kv]
    return pl.pallas_call(
        functools.partial(block_kernel, tick),
        out_shape=like(
            ((half, width), jnp.float32),
            ((half - half // CHIPS, width), jnp.bfloat16),
            ((half // CHIPS, width), jnp.bfloat16),
            (kv.shape, jnp.bfloat16),
        ),
        in_specs=[SCALARS] * 2 + [WHOLE] * (len(args) - 2),
        out_specs=(WHOLE,) * 4,
        scratch_shapes=[
            VMEM((2 * half, width), jnp.bfloat16),
            VMEM((2 * half, columns), jnp.bfloat16),
        ],
        input_output_aliases={len(args) - 1: 3},
        compiler_params=params(8),
        cost_estimate=pl.CostEstimate(
            flops=16 * half * columns * width,
            bytes_accessed=8 * columns * width,
            transcendentals=0,
        ),
        name="block",
    )(*args)


def split_last_kernel(kept, came, out):
    rows = out.shape[0]
    out[...] = (kept[-rows:, :] + f32(came[...])).astype(jnp.bfloat16)


def split_last(kept, came):
    return pl.pallas_call(
        split_last_kernel,
        out_shape=jax.ShapeDtypeStruct(came.shape, jnp.bfloat16),
        in_specs=[WHOLE] * 2,
        out_specs=WHOLE,
        compiler_params=params(4),
        name="split_last",
    )(kept, came)


def split_kernel(kept, came, mine, *others):
    rows = mine.shape[0]
    mine[...] = kept[:rows, :] + f32(came[:rows, :])
    for place, out in enumerate(others):
        part = slice((place + 1) * rows, (place + 2) * rows)
        out[...] = (kept[part, :] + f32(came[part, :])).astype(jnp.bfloat16)


def split(kept, came):
    shape = (kept.shape[0] // CHIPS, kept.shape[1])
    return pl.pallas_call(
        split_kernel,
        out_shape=like((shape, jnp.float32), *[(shape, jnp.bfloat16)] * (CHIPS - 2)),
        in_specs=[WHOLE] * 2,
        out_specs=(WHOLE,) * (CHIPS - 1),
        compiler_params=params(4),
        name="split",
    )(kept, came)


def finish_kernel(first_tick, *refs):
    (section, mine, one, two, three), refs = refs[:5], refs[5:]
    mod, final_mod, w_final, w_embed, packet = refs[-5:]
    width, channels = w_embed.shape[1], w_embed.shape[0]
    hidden, latent = refs[:2]
    if not first_tick:
        latent = latent.at[:, width : width + channels]
    last = mod.shape[1] - 1
    here = section[0]
    total = mine[...] + f32(one[...]) + f32(two[...]) + f32(three[...])
    gate = mod[2, pl.ds(here, 1), :]
    result = (f32(hidden[...]) + gate * total).astype(jnp.bfloat16)

    @pl.when(here == last)
    def _():
        normed = layer_norm(f32(result), final_mod[0:1, :], final_mod[1:2, :])
        velocity = dot_rows(normed, w_final[...])
        fresh = (f32(latent[...]) + velocity).astype(jnp.bfloat16)
        packet[:, width : width + channels] = fresh

    @pl.when(here != last)
    def _():
        packet[:, :width] = result
        packet[:, width : width + channels] = latent[...]


def finish(section, parts, state, mod, final_mod, w_final, w_embed):
    rows, width = parts[0].shape
    args = [*parts, *state, mod, final_mod, w_final, w_embed]
    return pl.pallas_call(
        functools.partial(finish_kernel, state[1].shape[1] == w_embed.shape[0]),
        out_shape=jax.ShapeDtypeStruct((rows, width + LANES), jnp.bfloat16),
        in_specs=[SCALARS] + [WHOLE] * len(args),
        out_specs=WHOLE,
        compiler_params=params(4),
        name="finish",
    )(section, *args)


def arrive(section, packet, w_embed, hidden):
    width, channels = w_embed.shape[1], w_embed.shape[0]

    @pl.when(section[0] == 0)
    def _():
        latent = packet[:, width : width + channels]
        hidden[...] = dot(latent, w_embed[...]).astype(jnp.bfloat16)

    @pl.when(section[0] != 0)
    def _():
        hidden[...] = packet[:, :width]


def norm_kernel(section, packet, mod, w_embed, hidden, normed):
    arrive(section, packet, w_embed, hidden)
    normed[...] = norm_here(section, f32(hidden[...]), mod)


def norm(section, packet, mod, w_embed):
    shape = ((packet.shape[0], mod.shape[2]), jnp.bfloat16)
    return pl.pallas_call(
        norm_kernel,
        out_shape=like(shape, shape),
        in_specs=[SCALARS] + [WHOLE] * 3,
        out_specs=(WHOLE,) * 2,
        compiler_params=params(4),
        name="norm",
    )(section, packet, mod, w_embed)


def load_kernel(count, *refs):
    sources, targets, semaphores = refs[:count], refs[count : 2 * count], refs[2 * count :]
    parts, _, columns = sources[0].shape
    copies = [
        pltpu.make_async_copy(
            sources[0].at[part],
            targets[0].at[:, part * columns : (part + 1) * columns],
            semaphores[count + part],
        )
        for part in range(parts)
    ]
    rest = zip(sources[1:], targets[1:], semaphores[1:count])
    copies += [pltpu.make_async_copy(*each) for each in rest]
    for copy in copies:
        copy.start()
    for copy in copies:
        copy.wait()


def load(*arrays):
    count = len(arrays)
    parts, depth, columns = arrays[0].shape
    shapes = [(depth, parts * columns)] + [array.shape for array in arrays[1:]]
    size = sum(array.size * array.dtype.itemsize for array in arrays)
    return pl.pallas_call(
        functools.partial(load_kernel, count),
        out_shape=tuple(VMEM(shape, array.dtype) for shape, array in zip(shapes, arrays)),
        in_specs=[pl.BlockSpec(memory_space=pltpu.HBM)] * count,
        out_specs=(WHOLE,) * count,
        scratch_shapes=[pltpu.SemaphoreType.DMA(())] * (count + parts),
        compiler_params=params(60 - -(-size >> 20)),
        cost_estimate=pl.CostEstimate(flops=0, bytes_accessed=2 * size, transcendentals=0),
        name="load",
    )(*arrays)


def open_kernel(section, packet, w_embed, hidden, latent):
    width = hidden.shape[1]
    arrive(section, packet, w_embed, hidden)
    latent[...] = packet[:, width : width + latent.shape[1]]


def open_packet(section, packet, w_embed):
    channels, width = w_embed.shape
    return pl.pallas_call(
        open_kernel,
        out_shape=like(
            ((packet.shape[0], width), jnp.bfloat16), ((packet.shape[0], channels), jnp.bfloat16)
        ),
        in_specs=[SCALARS] + [WHOLE] * 2,
        out_specs=(WHOLE,) * 2,
        compiler_params=params(4),
        name="open",
    )(section, packet, w_embed)


def exchange(value, apart):
    route = [(device, device ^ apart) for device in range(lax.axis_size("section"))]
    return lax.ppermute(value, "section", route)


def gather_chips(rows):
    return [rows] + [exchange(rows, apart) for apart in CHIP_STEPS]


def body(
    hidden_in,
    latent_in,
    w_qkv,
    w_out,
    stale_kv,
    qk_gain,
    block_mod,
    final_mod,
    w_final,
    w_embed,
    patch_flow,
):
    size = lax.axis_size("section")
    ticks = patch_flow.shape[0]
    section = (lax.axis_index("section") // GROUP).astype(jnp.int32).reshape(1)
    w_final = jnp.transpose(w_final)
    onward = [(device, (device + GROUP) % size) for device in range(size)]
    across = [(device, target ^ (GROUP // 2)) for device, target in onward]

    mod = jnp.transpose(block_mod, (1, 0, 2))
    held = load(w_qkv, w_out, qk_gain, jnp.transpose(patch_flow), stale_kv, mod)
    section, normed = lax.optimization_barrier((section, hidden_in))
    state = (hidden_in, latent_in)
    for tick in range(ticks):
        if tick > 0:
            hidden, normed = norm(section, packet, mod, w_embed)
            state = (hidden, packet)
        own = gather_chips(normed)
        if tick == 0:
            own, w_qkv, w_out, gains, patch_flow, kv, mod = lax.optimization_barrier((own, *held))
        pieces = own + [exchange(piece, 1) for piece in own]
        kept, sent, ahead, kv = block(tick, section, patch_flow, pieces, mod, gains, w_qkv, w_out, kv)
        crossed = exchange(ahead, 1)
        came = exchange(sent, 1)
        ahead = split_last(kept, crossed)
        mine, *blocks = split(kept, came)
        came = [exchange(rows, apart) for rows, apart in zip([*blocks, ahead], CHIP_STEPS)]
        parts = [mine] + came[::-1]
        packet = finish(section, parts, state, mod, final_mod, w_final, w_embed)
        swaps = tick < ticks - ticks % 2
        packet = lax.ppermute(packet, "section", across if swaps else onward)
    return open_packet(section, packet, w_embed)


def solution(mesh):
    in_specs = (
        P(("groups", "section"), None),
        P(("groups", "section"), None),
        P(None, None, "section"),
        P("section", None),
        P("groups", None, "section"),
        P(),
        P("groups", None, None),
        P("groups", None),
        P(),
        P(),
        P(),
    )
    out_specs = (P(("groups", "section"), None), P(("groups", "section"), None))
    return jax.shard_map(body, mesh=mesh, in_specs=in_specs, out_specs=out_specs, check_vma=False)
```

```python
import functools
import math

import jax
import jax.numpy as jnp
from jax import lax
from jax.experimental import pallas as pl
from jax.experimental.pallas import tpu as pltpu
from jax.sharding import PartitionSpec as P


HS = 128
GROUP = 8
CHIPS = 4
CHIP_STEPS = (2, 4, 6)
LANES = 128
EPS = 1e-6
VMEM = pltpu.VMEM
WHOLE = pl.BlockSpec(memory_space=pltpu.VMEM)
SCALARS = pl.BlockSpec(memory_space=pltpu.SMEM)


def f32(value):
    return value.astype(jnp.float32)


def dot(left, right):
    return jnp.dot(left, right, preferred_element_type=jnp.float32)


def dot_rows(left, right):
    return lax.dot_general(
        left, right, (((1,), (1,)), ((), ())), preferred_element_type=jnp.float32
    )


def params(mebibytes):
    return pltpu.CompilerParams(vmem_limit_bytes=mebibytes * 1024 * 1024)


def like(*shapes):
    return tuple(jax.ShapeDtypeStruct(shape, dtype) for shape, dtype in shapes)


def layer_norm(tokens, offset_row, scale_row):
    average = jnp.mean(tokens, axis=-1, keepdims=True)
    centred = tokens - average
    variance = jnp.mean(centred * centred, axis=-1, keepdims=True)
    return (centred * lax.rsqrt(variance + EPS) * (1.0 + scale_row) + offset_row).astype(
        jnp.bfloat16
    )


def head_norm(values, gain_row):
    power = jnp.mean(values * values, axis=-1, keepdims=True)
    return (values * lax.rsqrt(power + EPS) * gain_row).astype(jnp.bfloat16)


def norm_here(section, tokens, mod):
    here = section[0]
    return layer_norm(tokens, mod[0, pl.ds(here, 1), :], mod[1, pl.ds(here, 1), :])


def block_kernel(tick, section, patch_flow, *refs):
    pieces, refs = refs[: 2 * CHIPS], refs[2 * CHIPS :]
    if tick == 0:
        mod, refs = refs[0], refs[1:]
    gains, w_qkv, w_out, _, kept, sent, ahead, kv, normed, mixed = refs
    part_rows, width = pieces[0].shape
    half = CHIPS * part_rows
    rows = 2 * half
    heads = w_out.shape[0] // HS
    here = section[0]
    for place, piece in enumerate(pieces):
        values = piece[...]
        if tick == 0:
            values = norm_here(section, f32(values), mod)
        normed[place * part_rows : (place + 1) * part_rows, :] = values
    start = pl.multiple_of(patch_flow[here, tick] * rows, rows)
    gain = gains[here]
    tokens = normed[...]
    columns = w_out.shape[0]
    products = dot(tokens, w_qkv[...])
    queries, keys = products[:, :columns], products[:, columns : 2 * columns]
    for head in range(heads):
        part = slice(head * HS, (head + 1) * HS)
        kv[0, pl.ds(start, rows), part] = head_norm(keys[:, part], gain[1:2, :])
    kv[1, pl.ds(start, rows), :] = products[:, 2 * columns :].astype(jnp.bfloat16)
    for head in range(heads):
        part = slice(head * HS, (head + 1) * HS)
        query = head_norm(queries[:, part], gain[0:1, :])
        weights = jnp.exp(dot_rows(query, kv[0, :, part]) / math.sqrt(HS))
        totals = jnp.sum(weights, axis=-1, keepdims=True)
        attended = dot(weights.astype(jnp.bfloat16), kv[1, :, part])
        mixed[:, part] = (attended / totals).astype(jnp.bfloat16)
    tile = width // 4
    heads_out = mixed[...]
    edge = rows - half // CHIPS
    for low in range(0, width, tile):
        projected = dot(heads_out, w_out[:, low : low + tile])
        kept[:, low : low + tile] = projected[:half, :]
        sent[:, low : low + tile] = projected[half:edge, :].astype(jnp.bfloat16)
        ahead[:, low : low + tile] = projected[edge:, :].astype(jnp.bfloat16)


def block(tick, section, patch_flow, pieces, mod, gains, w_qkv, w_out, kv):
    half, width = CHIPS * pieces[0].shape[0], pieces[0].shape[1]
    columns = w_out.shape[0]
    args = [section, patch_flow, *pieces] + [mod] * (tick == 0) + [gains, w_qkv, w_out, kv]
    return pl.pallas_call(
        functools.partial(block_kernel, tick),
        out_shape=like(
            ((half, width), jnp.float32),
            ((half - half // CHIPS, width), jnp.bfloat16),
            ((half // CHIPS, width), jnp.bfloat16),
        )
        + (VMEM(kv.shape, kv.dtype),),
        in_specs=[SCALARS] * 2 + [WHOLE] * (len(args) - 2),
        out_specs=(WHOLE,) * 4,
        scratch_shapes=[
            VMEM((2 * half, width), jnp.bfloat16),
            VMEM((2 * half, columns), jnp.bfloat16),
        ],
        input_output_aliases={len(args) - 1: 3},
        compiler_params=params(8),
        cost_estimate=pl.CostEstimate(
            flops=16 * half * columns * width,
            bytes_accessed=8 * columns * width,
            transcendentals=0,
        ),
        name="block",
    )(*args)


def split_last_kernel(kept, came, out):
    rows = out.shape[0]
    out[...] = (kept[-rows:, :] + f32(came[...])).astype(jnp.bfloat16)


def split_last(kept, came):
    return pl.pallas_call(
        split_last_kernel,
        out_shape=jax.ShapeDtypeStruct(came.shape, jnp.bfloat16),
        in_specs=[WHOLE] * 2,
        out_specs=WHOLE,
        compiler_params=params(4),
        name="split_last",
    )(kept, came)


def split_kernel(kept, came, mine, *others):
    rows = mine.shape[0]
    mine[...] = kept[:rows, :] + f32(came[:rows, :])
    for place, out in enumerate(others):
        part = slice((place + 1) * rows, (place + 2) * rows)
        out[...] = (kept[part, :] + f32(came[part, :])).astype(jnp.bfloat16)


def split(kept, came):
    shape = (kept.shape[0] // CHIPS, kept.shape[1])
    return pl.pallas_call(
        split_kernel,
        out_shape=like((shape, jnp.float32), *[(shape, jnp.bfloat16)] * (CHIPS - 2)),
        in_specs=[WHOLE] * 2,
        out_specs=(WHOLE,) * (CHIPS - 1),
        compiler_params=params(4),
        name="split",
    )(kept, came)


def finish_kernel(first_tick, *refs):
    (section, mine, one, two, three), refs = refs[:5], refs[5:]
    mod, final_mod, w_final, w_embed, packet = refs[-5:]
    width, channels = w_embed.shape[1], w_embed.shape[0]
    hidden, latent = refs[:2]
    if not first_tick:
        latent = latent.at[:, width : width + channels]
    last = mod.shape[1] - 1
    here = section[0]
    total = mine[...] + f32(one[...]) + f32(two[...]) + f32(three[...])
    gate = mod[2, pl.ds(here, 1), :]
    result = (f32(hidden[...]) + gate * total).astype(jnp.bfloat16)

    @pl.when(here == last)
    def _():
        normed = layer_norm(f32(result), final_mod[0:1, :], final_mod[1:2, :])
        velocity = dot_rows(normed, w_final[...])
        fresh = (f32(latent[...]) + velocity).astype(jnp.bfloat16)
        packet[:, width : width + channels] = fresh

    @pl.when(here != last)
    def _():
        packet[:, :width] = result
        packet[:, width : width + channels] = latent[...]


def finish(section, parts, state, mod, final_mod, w_final, w_embed):
    rows, width = parts[0].shape
    args = [*parts, *state, mod, final_mod, w_final, w_embed]
    return pl.pallas_call(
        functools.partial(finish_kernel, state[1].shape[1] == w_embed.shape[0]),
        out_shape=jax.ShapeDtypeStruct((rows, width + LANES), jnp.bfloat16),
        in_specs=[SCALARS] + [WHOLE] * len(args),
        out_specs=WHOLE,
        compiler_params=params(4),
        name="finish",
    )(section, *args)


def arrive(section, packet, w_embed, hidden):
    width, channels = w_embed.shape[1], w_embed.shape[0]

    @pl.when(section[0] == 0)
    def _():
        latent = packet[:, width : width + channels]
        hidden[...] = dot(latent, w_embed[...]).astype(jnp.bfloat16)

    @pl.when(section[0] != 0)
    def _():
        hidden[...] = packet[:, :width]


def norm_kernel(section, packet, mod, w_embed, hidden, normed):
    arrive(section, packet, w_embed, hidden)
    normed[...] = norm_here(section, f32(hidden[...]), mod)


def norm(section, packet, mod, w_embed):
    shape = ((packet.shape[0], mod.shape[2]), jnp.bfloat16)
    return pl.pallas_call(
        norm_kernel,
        out_shape=like(shape, shape),
        in_specs=[SCALARS] + [WHOLE] * 3,
        out_specs=(WHOLE,) * 2,
        compiler_params=params(4),
        name="norm",
    )(section, packet, mod, w_embed)


def load_kernel(count, *refs):
    sources, targets, semaphores = refs[:count], refs[count : 2 * count], refs[2 * count :]
    parts, _, columns = sources[0].shape
    copies = [
        pltpu.make_async_copy(
            sources[0].at[part],
            targets[0].at[:, part * columns : (part + 1) * columns],
            semaphores[count + part],
        )
        for part in range(parts)
    ]
    rest = zip(sources[1:], targets[1:], semaphores[1:count])
    copies += [pltpu.make_async_copy(*each) for each in rest]
    for copy in copies:
        copy.start()
    for copy in copies:
        copy.wait()


def load(*arrays):
    count = len(arrays)
    parts, depth, columns = arrays[0].shape
    shapes = [(depth, parts * columns)] + [array.shape for array in arrays[1:]]
    size = sum(array.size * array.dtype.itemsize for array in arrays)
    return pl.pallas_call(
        functools.partial(load_kernel, count),
        out_shape=tuple(VMEM(shape, array.dtype) for shape, array in zip(shapes, arrays)),
        in_specs=[pl.BlockSpec(memory_space=pltpu.HBM)] * count,
        out_specs=(WHOLE,) * count,
        scratch_shapes=[pltpu.SemaphoreType.DMA(())] * (count + parts),
        compiler_params=params(60 - -(-size >> 20)),
        cost_estimate=pl.CostEstimate(flops=0, bytes_accessed=2 * size, transcendentals=0),
        name="load",
    )(*arrays)


def open_kernel(section, packet, w_embed, hidden, latent):
    width = hidden.shape[1]
    arrive(section, packet, w_embed, hidden)
    latent[...] = packet[:, width : width + latent.shape[1]]


def open_packet(section, packet, w_embed):
    channels, width = w_embed.shape
    return pl.pallas_call(
        open_kernel,
        out_shape=like(
            ((packet.shape[0], width), jnp.bfloat16), ((packet.shape[0], channels), jnp.bfloat16)
        ),
        in_specs=[SCALARS] + [WHOLE] * 2,
        out_specs=(WHOLE,) * 2,
        compiler_params=params(4),
        name="open",
    )(section, packet, w_embed)


def exchange(value, apart):
    route = [(device, device ^ apart) for device in range(lax.axis_size("section"))]
    return lax.ppermute(value, "section", route)


def gather_chips(rows):
    return [rows] + [exchange(rows, apart) for apart in CHIP_STEPS]


def body(
    hidden_in,
    latent_in,
    w_qkv,
    w_out,
    stale_kv,
    qk_gain,
    block_mod,
    final_mod,
    w_final,
    w_embed,
    patch_flow,
):
    size = lax.axis_size("section")
    ticks = patch_flow.shape[0]
    section = (lax.axis_index("section") // GROUP).astype(jnp.int32).reshape(1)
    w_final = jnp.transpose(w_final)
    onward = [(device, (device + GROUP) % size) for device in range(size)]
    across = [(device, target ^ (GROUP // 2)) for device, target in onward]

    mod = jnp.transpose(block_mod, (1, 0, 2))
    held = load(w_qkv, w_out, qk_gain, jnp.transpose(patch_flow), stale_kv, mod)
    section, normed = lax.optimization_barrier((section, hidden_in))
    state = (hidden_in, latent_in)
    for tick in range(ticks):
        if tick > 0:
            hidden, normed = norm(section, packet, mod, w_embed)
            state = (hidden, packet)
        own = gather_chips(normed)
        if tick == 0:
            own, w_qkv, w_out, gains, patch_flow, kv, mod = lax.optimization_barrier((own, *held))
        pieces = own + [exchange(piece, 1) for piece in own]
        kept, sent, ahead, kv = block(tick, section, patch_flow, pieces, mod, gains, w_qkv, w_out, kv)
        crossed = exchange(ahead, 1)
        came = exchange(sent, 1)
        ahead = split_last(kept, crossed)
        mine, *blocks = split(kept, came)
        came = [exchange(rows, apart) for rows, apart in zip([*blocks, ahead], CHIP_STEPS)]
        parts = [mine] + came[::-1]
        packet = finish(section, parts, state, mod, final_mod, w_final, w_embed)
        swaps = tick < ticks - ticks % 2
        packet = lax.ppermute(packet, "section", across if swaps else onward)
    return open_packet(section, packet, w_embed)


def solution(mesh):
    in_specs = (
        P(("groups", "section"), None),
        P(("groups", "section"), None),
        P(None, None, "section"),
        P("section", None),
        P("groups", None, "section"),
        P(),
        P("groups", None, None),
        P("groups", None),
        P(),
        P(),
        P(),
    )
    out_specs = (P(("groups", "section"), None), P(("groups", "section"), None))
    return jax.shard_map(body, mesh=mesh, in_specs=in_specs, out_specs=out_specs, check_vma=False)
```

```python
import functools
import math

import jax
import jax.numpy as jnp
from jax import lax
from jax.experimental import pallas as pl
from jax.experimental.pallas import tpu as pltpu
from jax.sharding import PartitionSpec as P


HS = 128
GROUP = 8
CHIPS = 4
CHIP_STEPS = (2, 4, 6)
LANES = 128
EPS = 1e-6
VMEM = pltpu.VMEM
WHOLE = pl.BlockSpec(memory_space=pltpu.VMEM)
SCALARS = pl.BlockSpec(memory_space=pltpu.SMEM)


def f32(value):
    return value.astype(jnp.float32)


def dot(left, right):
    return jnp.dot(left, right, preferred_element_type=jnp.float32)


def dot_rows(left, right):
    return lax.dot_general(
        left, right, (((1,), (1,)), ((), ())), preferred_element_type=jnp.float32
    )


def params(mebibytes):
    return pltpu.CompilerParams(vmem_limit_bytes=mebibytes * 1024 * 1024)


def like(*shapes):
    return tuple(jax.ShapeDtypeStruct(shape, dtype) for shape, dtype in shapes)


def layer_norm(tokens, offset_row, scale_row):
    average = jnp.mean(tokens, axis=-1, keepdims=True)
    centred = tokens - average
    variance = jnp.mean(centred * centred, axis=-1, keepdims=True)
    return (centred * lax.rsqrt(variance + EPS) * (1.0 + scale_row) + offset_row).astype(
        jnp.bfloat16
    )


def head_norm(values, gain_row):
    power = jnp.mean(values * values, axis=-1, keepdims=True)
    return (values * lax.rsqrt(power + EPS) * gain_row).astype(jnp.bfloat16)


def norm_here(section, tokens, mod):
    here = section[0]
    return layer_norm(tokens, mod[0, pl.ds(here, 1), :], mod[1, pl.ds(here, 1), :])


def block_kernel(tick, section, patch_flow, *refs):
    pieces, refs = refs[: 2 * CHIPS], refs[2 * CHIPS :]
    if tick == 0:
        mod, refs = refs[0], refs[1:]
    gains, w_qkv, w_out, _, kept, sent, ahead, kv, mixed = refs
    part_rows, width = pieces[0].shape
    half = CHIPS * part_rows
    rows = 2 * half
    heads = w_out.shape[0] // HS
    here = section[0]
    values_of = []
    for piece in pieces:
        values = piece[...]
        if tick == 0:
            values = norm_here(section, f32(values), mod)
        values_of.append(values)
    start = pl.multiple_of(patch_flow[here, tick] * rows, rows)
    gain = gains[here]
    tokens = jnp.concatenate(values_of, 0)
    columns = w_out.shape[0]
    products = dot(tokens, w_qkv[...])
    queries, keys = products[:, :columns], products[:, columns : 2 * columns]
    for head in range(heads):
        part = slice(head * HS, (head + 1) * HS)
        kv[0, pl.ds(start, rows), part] = head_norm(keys[:, part], gain[1:2, :])
    kv[1, pl.ds(start, rows), :] = products[:, 2 * columns :].astype(jnp.bfloat16)
    for head in range(heads):
        part = slice(head * HS, (head + 1) * HS)
        query = head_norm(queries[:, part], gain[0:1, :])
        weights = jnp.exp(dot_rows(query, kv[0, :, part]) / math.sqrt(HS))
        totals = jnp.sum(weights, axis=-1, keepdims=True)
        attended = dot(weights.astype(jnp.bfloat16), kv[1, :, part])
        mixed[:, part] = (attended / totals).astype(jnp.bfloat16)
    tile = width // 4
    heads_out = mixed[...]
    edge = rows - half // CHIPS
    for low in range(0, width, tile):
        projected = dot(heads_out, w_out[:, low : low + tile])
        kept[:, low : low + tile] = projected[:half, :]
        sent[:, low : low + tile] = projected[half:edge, :].astype(jnp.bfloat16)
        ahead[:, low : low + tile] = projected[edge:, :].astype(jnp.bfloat16)


def block(tick, section, patch_flow, pieces, mod, gains, w_qkv, w_out, kv):
    half, width = CHIPS * pieces[0].shape[0], pieces[0].shape[1]
    columns = w_out.shape[0]
    args = [section, patch_flow, *pieces] + [mod] * (tick == 0) + [gains, w_qkv, w_out, kv]
    return pl.pallas_call(
        functools.partial(block_kernel, tick),
        out_shape=like(
            ((half, width), jnp.float32),
            ((half - half // CHIPS, width), jnp.bfloat16),
            ((half // CHIPS, width), jnp.bfloat16),
        )
        + (VMEM(kv.shape, kv.dtype),),
        in_specs=[SCALARS] * 2 + [WHOLE] * (len(args) - 2),
        out_specs=(WHOLE,) * 4,
        scratch_shapes=[
            VMEM((2 * half, columns), jnp.bfloat16),
        ],
        input_output_aliases={len(args) - 1: 3},
        compiler_params=params(8),
        cost_estimate=pl.CostEstimate(
            flops=16 * half * columns * width,
            bytes_accessed=8 * columns * width,
            transcendentals=0,
        ),
        name="block",
    )(*args)


def split_last_kernel(kept, came, out):
    rows = out.shape[0]
    out[...] = (kept[-rows:, :] + f32(came[...])).astype(jnp.bfloat16)


def split_last(kept, came):
    return pl.pallas_call(
        split_last_kernel,
        out_shape=jax.ShapeDtypeStruct(came.shape, jnp.bfloat16),
        in_specs=[WHOLE] * 2,
        out_specs=WHOLE,
        compiler_params=params(4),
        name="split_last",
    )(kept, came)


def split_kernel(kept, came, mine, *others):
    rows = mine.shape[0]
    mine[...] = kept[:rows, :] + f32(came[:rows, :])
    for place, out in enumerate(others):
        part = slice((place + 1) * rows, (place + 2) * rows)
        out[...] = (kept[part, :] + f32(came[part, :])).astype(jnp.bfloat16)


def split(kept, came):
    shape = (kept.shape[0] // CHIPS, kept.shape[1])
    return pl.pallas_call(
        split_kernel,
        out_shape=like((shape, jnp.float32), *[(shape, jnp.bfloat16)] * (CHIPS - 2)),
        in_specs=[WHOLE] * 2,
        out_specs=(WHOLE,) * (CHIPS - 1),
        compiler_params=params(4),
        name="split",
    )(kept, came)


def finish_kernel(first_tick, *refs):
    (section, mine, one, two, three), refs = refs[:5], refs[5:]
    mod, final_mod, w_final, w_embed, packet = refs[-5:]
    width, channels = w_embed.shape[1], w_embed.shape[0]
    hidden, latent = refs[:2]
    if not first_tick:
        latent = latent.at[:, width : width + channels]
    last = mod.shape[1] - 1
    here = section[0]
    total = mine[...] + f32(one[...]) + f32(two[...]) + f32(three[...])
    gate = mod[2, pl.ds(here, 1), :]
    result = (f32(hidden[...]) + gate * total).astype(jnp.bfloat16)

    @pl.when(here == last)
    def _():
        normed = layer_norm(f32(result), final_mod[0:1, :], final_mod[1:2, :])
        velocity = dot_rows(normed, w_final[...])
        fresh = (f32(latent[...]) + velocity).astype(jnp.bfloat16)
        packet[:, width : width + channels] = fresh

    @pl.when(here != last)
    def _():
        packet[:, :width] = result
        packet[:, width : width + channels] = latent[...]


def finish(section, parts, state, mod, final_mod, w_final, w_embed):
    rows, width = parts[0].shape
    args = [*parts, *state, mod, final_mod, w_final, w_embed]
    return pl.pallas_call(
        functools.partial(finish_kernel, state[1].shape[1] == w_embed.shape[0]),
        out_shape=jax.ShapeDtypeStruct((rows, width + LANES), jnp.bfloat16),
        in_specs=[SCALARS] + [WHOLE] * len(args),
        out_specs=WHOLE,
        compiler_params=params(4),
        name="finish",
    )(section, *args)


def arrive(section, packet, w_embed, hidden):
    width, channels = w_embed.shape[1], w_embed.shape[0]

    @pl.when(section[0] == 0)
    def _():
        latent = packet[:, width : width + channels]
        hidden[...] = dot(latent, w_embed[...]).astype(jnp.bfloat16)

    @pl.when(section[0] != 0)
    def _():
        hidden[...] = packet[:, :width]


def norm_kernel(section, packet, mod, w_embed, hidden, normed):
    arrive(section, packet, w_embed, hidden)
    normed[...] = norm_here(section, f32(hidden[...]), mod)


def norm(section, packet, mod, w_embed):
    shape = ((packet.shape[0], mod.shape[2]), jnp.bfloat16)
    return pl.pallas_call(
        norm_kernel,
        out_shape=like(shape, shape),
        in_specs=[SCALARS] + [WHOLE] * 3,
        out_specs=(WHOLE,) * 2,
        compiler_params=params(4),
        name="norm",
    )(section, packet, mod, w_embed)


def load_kernel(count, *refs):
    sources, targets, semaphores = refs[:count], refs[count : 2 * count], refs[2 * count :]
    parts, _, columns = sources[0].shape
    copies = [
        pltpu.make_async_copy(
            sources[0].at[part],
            targets[0].at[:, part * columns : (part + 1) * columns],
            semaphores[count + part],
        )
        for part in range(parts)
    ]
    rest = zip(sources[1:], targets[1:], semaphores[1:count])
    copies += [pltpu.make_async_copy(*each) for each in rest]
    for copy in copies:
        copy.start()
    for copy in copies:
        copy.wait()


def load(*arrays):
    count = len(arrays)
    parts, depth, columns = arrays[0].shape
    shapes = [(depth, parts * columns)] + [array.shape for array in arrays[1:]]
    size = sum(array.size * array.dtype.itemsize for array in arrays)
    return pl.pallas_call(
        functools.partial(load_kernel, count),
        out_shape=tuple(VMEM(shape, array.dtype) for shape, array in zip(shapes, arrays)),
        in_specs=[pl.BlockSpec(memory_space=pltpu.HBM)] * count,
        out_specs=(WHOLE,) * count,
        scratch_shapes=[pltpu.SemaphoreType.DMA(())] * (count + parts),
        compiler_params=params(60 - -(-size >> 20)),
        cost_estimate=pl.CostEstimate(flops=0, bytes_accessed=2 * size, transcendentals=0),
        name="load",
    )(*arrays)


def open_kernel(section, packet, w_embed, hidden, latent):
    width = hidden.shape[1]
    arrive(section, packet, w_embed, hidden)
    latent[...] = packet[:, width : width + latent.shape[1]]


def open_packet(section, packet, w_embed):
    channels, width = w_embed.shape
    return pl.pallas_call(
        open_kernel,
        out_shape=like(
            ((packet.shape[0], width), jnp.bfloat16), ((packet.shape[0], channels), jnp.bfloat16)
        ),
        in_specs=[SCALARS] + [WHOLE] * 2,
        out_specs=(WHOLE,) * 2,
        compiler_params=params(4),
        name="open",
    )(section, packet, w_embed)


def exchange(value, apart):
    route = [(device, device ^ apart) for device in range(lax.axis_size("section"))]
    return lax.ppermute(value, "section", route)


def gather_chips(rows):
    return [rows] + [exchange(rows, apart) for apart in CHIP_STEPS]


def body(
    hidden_in,
    latent_in,
    w_qkv,
    w_out,
    stale_kv,
    qk_gain,
    block_mod,
    final_mod,
    w_final,
    w_embed,
    patch_flow,
):
    size = lax.axis_size("section")
    ticks = patch_flow.shape[0]
    section = (lax.axis_index("section") // GROUP).astype(jnp.int32).reshape(1)
    w_final = jnp.transpose(w_final)
    onward = [(device, (device + GROUP) % size) for device in range(size)]
    across = [(device, target ^ (GROUP // 2)) for device, target in onward]

    mod = jnp.transpose(block_mod, (1, 0, 2))
    held = load(w_qkv, w_out, qk_gain, jnp.transpose(patch_flow), stale_kv, mod)
    section, normed = lax.optimization_barrier((section, hidden_in))
    state = (hidden_in, latent_in)
    for tick in range(ticks):
        if tick > 0:
            hidden, normed = norm(section, packet, mod, w_embed)
            state = (hidden, packet)
        own = gather_chips(normed)
        if tick == 0:
            own, w_qkv, w_out, gains, patch_flow, kv, mod = lax.optimization_barrier((own, *held))
        pieces = own + [exchange(piece, 1) for piece in own]
        kept, sent, ahead, kv = block(tick, section, patch_flow, pieces, mod, gains, w_qkv, w_out, kv)
        crossed = exchange(ahead, 1)
        came = exchange(sent, 1)
        ahead = split_last(kept, crossed)
        mine, *blocks = split(kept, came)
        came = [exchange(rows, apart) for rows, apart in zip([*blocks, ahead], CHIP_STEPS)]
        parts = [mine] + came[::-1]
        packet = finish(section, parts, state, mod, final_mod, w_final, w_embed)
        swaps = tick < ticks - ticks % 2
        packet = lax.ppermute(packet, "section", across if swaps else onward)
    return open_packet(section, packet, w_embed)


def solution(mesh):
    in_specs = (
        P(("groups", "section"), None),
        P(("groups", "section"), None),
        P(None, None, "section"),
        P("section", None),
        P("groups", None, "section"),
        P(),
        P("groups", None, None),
        P("groups", None),
        P(),
        P(),
        P(),
    )
    out_specs = (P(("groups", "section"), None), P(("groups", "section"), None))
    return jax.shard_map(body, mesh=mesh, in_specs=in_specs, out_specs=out_specs, check_vma=False)
```
